32 devices in a mesh: docs: 8 (over z, x), heads: 4 (over y, core).
Axes of the slice: x: 2, y: 2, z: 4, core: 2. Of those that a mesh axis runs over, the one named last changes fastest.
Arguments:
- tokens: bfloat16 [10240, 768], P('docs'), may hold values from -6 to 6
- seg_index: int32 [16, 512], P('docs'), may hold values from 0 to 127, as said below
- seg_count: int32 [16], P('docs'), may hold values from 5 to 128, as said below
- weight_query: float32 [768, 768], P('docs', 'heads'), may hold values from -0.21875 to 0.21875
- weight_key: float32 [768, 768], P('docs', 'heads'), may hold values from -0.21875 to 0.21875
- weight_value: float32 [768, 768], P('docs', 'heads'), may hold values from -0.21875 to 0.21875
- weight_out: float32 [768, 768], P('heads', 'docs'), may hold values from -3.5 to 3.5
- weight_up: float32 [768, 3072], P('docs', 'heads'), may hold values from -0.21875 to 0.21875
- weight_down: float32 [3072, 768], P('heads', 'docs'), may hold values from -0.109375 to 0.109375
- bias_query: float32 [768], P('heads'), may hold values from -3 to 3
- bias_value: float32 [768], P('heads'), may hold values from -3 to 3
- bias_out: float32 [768], replicated, may hold values from -2 to 2
- bias_up: float32 [3072], P('heads'), may hold values from -2 to 2
- bias_down: float32 [768], replicated, may hold values from -2 to 2
- gain_one: float32 [768], replicated, may hold values from 0.25 to 1.75
- shift_one: float32 [768], replicated, may hold values from -2 to 2
- gain_two: float32 [768], replicated, may hold values from 0.25 to 1.75
- shift_two: float32 [768], replicated, may hold values from -2 to 2
- cotangent: bfloat16 [10240, 768], P('docs'), may hold values from -6 to 6
Outputs:
- layer_out: bfloat16 [10240, 768], P(('docs', 'heads'))
- grad_tokens: bfloat16 [10240, 768], P('docs')
- gradient_weight_query: float32 [768, 768], P('docs', 'heads')
- gradient_weight_key: float32 [768, 768], P('docs', 'heads')
- gradient_weight_value: float32 [768, 768], P('docs', 'heads')
- gradient_weight_out: float32 [768, 768], P('heads', 'docs')
- gradient_weight_up: float32 [768, 3072], P('docs', 'heads')
- gradient_weight_down: float32 [3072, 768], P('heads', 'docs')
- gradient_bias_query: float32 [768], P('heads')
- gradient_bias_value: float32 [768], P('heads')
- gradient_bias_out: float32 [768], replicated
- gradient_bias_up: float32 [3072], P('heads')
- gradient_bias_down: float32 [768], replicated
- gradient_gain_one: float32 [768], replicated
- gradient_shift_one: float32 [768], replicated
- gradient_gain_two: float32 [768], replicated
- gradient_shift_two: float32 [768], replicated
The draws below stay inside these ranges and needn't reach their ends.
Inputs may be any that keep to these rules, and one draw needn't show every extreme that they name: `seg_count`: one document of each draw has exactly 128 segments. seg_index[d, t] is below seg_count[d]; the first text token of each document belongs to its last segment.
All inputs are finite; a program needn't handle non-finite values.
Results may differ from the reference program's by a relative error of at most 0.02.
Values may be sent and summed in bfloat16 or wider, within the bound.
No kernel may reach another device: no remote copies, remote signals or barrier semaphores. Data moves between devices by JAX's collectives and lax.ppermute only.
A program may use at most 128 MiB of HBM per device.

```python
import jax
import jax.numpy as jnp
from jax import lax

D = 768
HEADS = 12
HEAD_DIM = 64
FF = 3072
TEXT = 512
SLOTS = 128
LEN = 640
DOC_DEV = 2
DOCS = 16
TOKENS = 10240
N_DOCS = 8


def count_draw(key):
    uniform_ints = jax.random.randint(jax.random.fold_in(key, 7), (DOCS,), 0, SLOTS - 4)
    counts = 5 + uniform_ints * uniform_ints * uniform_ints // ((SLOTS - 4) * (SLOTS - 4))
    chosen = jax.random.randint(jax.random.fold_in(key, 9), (), 0, DOCS)
    return jnp.where(jnp.arange(DOCS) == chosen, SLOTS, counts).astype(jnp.int32)


def draw_seg_count(key, part):
    return count_draw(key)


def draw_seg_index(key, part):
    counts = count_draw(key)
    random_ints = jax.random.randint(jax.random.fold_in(key, 11), (DOCS, TEXT), 0, 1 << 20)
    segment_ids = random_ints % counts[:, None]
    leading = jnp.arange(TEXT)[None, :] == 0
    return jnp.where(leading, counts[:, None] - 1, segment_ids).astype(jnp.int32)


def spiked(entries, own_key, source, target, parts, factor):
    def block_of(axis_at):
        return (jnp.arange(entries.shape[axis_at]) // (entries.shape[axis_at] // parts)).reshape((-1,) + (1,) * (entries.ndim - 1 - axis_at))

    near = jax.random.permutation(own_key, parts)[block_of(target)]
    other_side = (block_of(target) + parts // 2) % parts
    return jnp.where((block_of(source) == near) | (block_of(source) == other_side), factor * entries, entries)


def block_levels(key, dims, cuts, low, high):
    level, own = 1.0, jax.random.fold_in(key, 6)
    for axis_at, shards_of in cuts:
        draws = jnp.exp(jax.random.uniform(jax.random.fold_in(own, axis_at), (shards_of,), jnp.float32, low / len(cuts), high / len(cuts)))
        level = level * jnp.repeat(draws, dims[axis_at] // shards_of).reshape([-1 if axis == axis_at else 1 for axis in range(len(dims))])
    return level


def normal_values(own_key, dims, scale, reach, split=(), held_as=jnp.bfloat16):
    entries = jax.random.normal(own_key, dims, jnp.float32) * scale
    if len(split) > 0:
        entries = block_levels(own_key, dims, split, -0.22, 0.18) * entries
    return jnp.clip(entries, min=-reach, max=reach).astype(held_as)


def heavy_noise(stream_key, extent, spread, most, cuts, heavy, kind=jnp.bfloat16):
    result = spread * jax.random.normal(stream_key, extent, jnp.float32)
    if cuts:
        result = result * block_levels(stream_key, extent, cuts, -0.22, 0.18)
    return jnp.clip(spiked(result, jax.random.fold_in(stream_key, 3), *heavy), -most, most).astype(kind)


def setup_inputs(seed: int = 0) -> dict:
    key_of = jax.random.split(jax.random.key(seed), 20)
    return {
        "tokens": normal_values(key_of[0], (TOKENS, D), 1.0, 6.0, ((0, 8),)),
        "seg_index": draw_seg_index(jax.random.fold_in(key_of[19], 71), 0),
        "seg_count": draw_seg_count(jax.random.fold_in(key_of[19], 71), 0),
        "weight_query": normal_values(key_of[3], (D, D), D ** -0.5, 0.21875, ((0, 8), (1, 4)), jnp.float32),
        "weight_key": normal_values(key_of[4], (D, D), D ** -0.5, 0.21875, ((0, 8), (1, 4)), jnp.float32),
        "weight_value": normal_values(key_of[5], (D, D), D ** -0.5, 0.21875, ((0, 8), (1, 4)), jnp.float32),
        "weight_out": normal_values(key_of[6], (D, D), (max(3 * D // LEN, 1)) ** -0.5, 3.5, ((0, 4), (1, 8)), jnp.float32),
        "weight_up": normal_values(key_of[7], (D, FF), D ** -0.5, 0.21875, ((0, 8), (1, 4)), jnp.float32),
        "weight_down": normal_values(key_of[8], (FF, D), FF ** -0.5, 0.109375, ((0, 4), (1, 8)), jnp.float32),
        "bias_query": normal_values(key_of[9], (D,), 0.5, 3.0, ((0, 4),), jnp.float32),
        "bias_value": normal_values(key_of[10], (D,), 0.5, 3.0, ((0, 4),), jnp.float32),
        "bias_out": normal_values(key_of[11], (D,), 0.3, 2.0, (), jnp.float32),
        "bias_up": normal_values(key_of[12], (FF,), 0.3, 2.0, ((0, 4),), jnp.float32),
        "bias_down": normal_values(key_of[13], (D,), 0.3, 2.0, (), jnp.float32),
        "gain_one": jnp.clip(1.0 + 0.15 * jax.random.normal(key_of[14], (D,), jnp.float32), 0.25, 1.75),
        "shift_one": normal_values(key_of[15], (D,), 0.3, 2.0, (), jnp.float32),
        "gain_two": jnp.clip(1.0 + 0.15 * jax.random.normal(key_of[16], (D,), jnp.float32), 0.25, 1.75),
        "shift_two": normal_values(key_of[17], (D,), 0.3, 2.0, (), jnp.float32),
        "cotangent": heavy_noise(key_of[18], (TOKENS, D), 1.0, 6.0, ((0, 8),), (0, 1, 8, 2.0)),
    }


@jax.custom_vjp
def low(v):
    return lax.optimization_barrier(v.astype(jnp.bfloat16)).astype(jnp.float32)

@jax.custom_vjp
def low_back(v):
    return v

def low_keep(v):
    return (low(v), None)

def low_pass(kept, grad):
    return (grad,)

def back_keep(v):
    return (v, None)

def back_low(kept, grad):
    return (low(grad),)
low.defvjp(low_keep, low_pass)
low_back.defvjp(back_keep, back_low)
epsilon = 1e-05
highest = lax.Precision.HIGHEST

def high_dot(left_side, right_side):
    return jnp.dot(left_side, right_side, precision=highest, preferred_element_type=jnp.float32)

def norm_rows(pre_rows, gain_vec, shift_vec):
    average = lax.optimization_barrier(jnp.mean(pre_rows, axis=-1, keepdims=True))
    centered = pre_rows - average
    variance = lax.optimization_barrier(jnp.mean(centered * centered, axis=-1, keepdims=True))
    return centered * lax.rsqrt(variance + epsilon) * gain_vec + shift_vec

def attend(pieces):
    queries, key_rows, value_rows, seg_total = pieces
    scores = jnp.einsum('qhd,khd->hqk', queries, key_rows, precision=highest) * HEAD_DIM ** (-0.5)
    scores = low_back(scores)
    visible = jnp.arange(LEN, dtype=jnp.int32) < TEXT + seg_total
    scores = jnp.where(visible[None, None, :], scores, -1000000000.0)
    probs_low = low(jax.nn.softmax(scores, axis=-1))
    return jnp.einsum('hqk,khd->qhd', probs_low, value_rows, precision=highest)

def layer_group(params, group_tokens, group_index, group_count):
    weight_query, weight_key, weight_value, weight_out, weight_up, weight_down, bias_query, bias_value, bias_out, bias_up, bias_down, gain_one, shift_one, gain_two, shift_two = params
    groups = group_count.shape[0]
    shaped = group_tokens.reshape(groups, LEN, D)
    text_rows = shaped[:, :TEXT]
    slot_ids = jnp.arange(SLOTS, dtype=jnp.int32)
    onehot = (group_index[:, :, None] == slot_ids[None, None, :]).astype(jnp.float32)
    members = lax.optimization_barrier(jnp.sum(onehot, axis=1))
    pooled = jnp.einsum('gts,gtd->gsd', onehot, text_rows, precision=highest)
    pooled = pooled / jnp.maximum(members, 1.0)[:, :, None]
    slot_live = (slot_ids[None, :] < group_count[:, None]).astype(jnp.float32)
    slot_rows = slot_live[:, :, None] * (shaped[:, TEXT:] + pooled)
    inputs = low_back(jnp.concatenate([text_rows, slot_rows], axis=1).reshape(groups * LEN, D))
    hidden_in = low(inputs)
    queries = low(low_back(high_dot(hidden_in, low(weight_query)) + bias_query))
    key_rows = low(low_back(high_dot(hidden_in, low(weight_key))))
    value_rows = low(low_back(high_dot(hidden_in, low(weight_value)) + bias_value))

    def to_heads(array):
        return array.reshape(groups, LEN, HEADS, HEAD_DIM)
    context = lax.map(jax.checkpoint(attend), (to_heads(queries), to_heads(key_rows), to_heads(value_rows), group_count))
    context = low(low_back(context.reshape(groups * LEN, D)))
    branch_one = low_back(high_dot(context, low(weight_out)) + bias_out)
    normed_one = norm_rows(inputs + branch_one, gain_one, shift_one)
    upward = low_back(high_dot(low(normed_one), low(weight_up)) + bias_up)
    activated = low(jax.nn.gelu(upward, approximate=False))
    branch_two = low_back(high_dot(activated, low(weight_down)) + bias_down)
    return norm_rows(normed_one + branch_two, gain_two, shift_two)

def reference(tokens, seg_index, seg_count, weight_query, weight_key, weight_value, weight_out, weight_up, weight_down, bias_query, bias_value, bias_out, bias_up, bias_down, gain_one, shift_one, gain_two, shift_two, cotangent):
    params = (weight_query, weight_key, weight_value, weight_out, weight_up, weight_down, bias_query, bias_value, bias_out, bias_up, bias_down, gain_one, shift_one, gain_two, shift_two)
    block_tokens = tokens.astype(jnp.float32).reshape(N_DOCS, DOC_DEV * LEN, D)
    block_cot = cotangent.astype(jnp.float32).reshape(N_DOCS, DOC_DEV * LEN, D)
    block_index = seg_index.reshape(N_DOCS, DOC_DEV, TEXT)
    block_count = seg_count.reshape(N_DOCS, DOC_DEV)

    def one_group(totals, pieces):
        group_tokens, group_index, group_count, group_cot = pieces

        def forward(param_set, rows_in):
            return layer_group(param_set, rows_in, group_index, group_count)
        group_out, pullback = jax.vjp(forward, params, group_tokens)
        grad_params, grad_rows = pullback(group_cot)
        totals = jax.tree.map(jnp.add, totals, grad_params)
        return (totals, (group_out, grad_rows))
    zero_grads = jax.tree.map(jnp.zeros_like, params)
    totals, (outputs, grad_rows) = lax.scan(one_group, zero_grads, (block_tokens, block_index, block_count, block_cot))
    layer_out = outputs.reshape(TOKENS, D).astype(jnp.bfloat16)
    grad_tokens = grad_rows.reshape(TOKENS, D).astype(jnp.bfloat16)
    return (layer_out, grad_tokens, totals[0], totals[1], totals[2], totals[3], totals[4], totals[5], totals[6], totals[7], totals[8], totals[9], totals[10], totals[11], totals[12], totals[13], totals[14])
```

```python
from functools import partial

import jax
import jax.numpy as jnp
from jax import lax
from jax.sharding import PartitionSpec as P

HEAD_DIM = 64


epsilon = 1e-05
masked_score = -1000000000.0


def norm_forward(pre_rows, gain_vec, shift_vec):
    average = jnp.mean(pre_rows, axis=-1, keepdims=True)
    centered = pre_rows - average
    variance = jnp.mean(centered * centered, axis=-1, keepdims=True)
    inv_std = lax.rsqrt(variance + epsilon)
    scaled = centered * inv_std
    return (scaled * gain_vec + shift_vec, scaled, inv_std)


def norm_backward(grad_out, scaled, inv_std, gain_vec):
    grad_scaled = grad_out * gain_vec
    mean_grad = jnp.mean(grad_scaled, axis=-1, keepdims=True)
    mean_along = jnp.mean(grad_scaled * scaled, axis=-1, keepdims=True)
    return inv_std * (grad_scaled - mean_grad - scaled * mean_along)


def contract_rows(left_side, right_side):
    return lax.dot_general(
        left_side, right_side, (((0,), (0,)), ((), ())), preferred_element_type=jnp.float32
    )


def contract_cols(left_side, right_side):
    return lax.dot_general(
        left_side, right_side, (((1,), (1,)), ((), ())), preferred_element_type=jnp.float32
    )


def score_block(queries, key_rows, seg_total, text_len):
    score_scale = HEAD_DIM ** (-0.5)
    scores = (
        jnp.einsum("hqd,hkd->hqk", queries, key_rows, preferred_element_type=jnp.float32)
        * score_scale
    )
    visible = jnp.arange(key_rows.shape[1], dtype=jnp.int32) < text_len + seg_total
    return jnp.where(visible[None, None, :], scores, masked_score)


def attend_forward(text_len, queries, key_rows, value_rows, seg_total):
    scores = score_block(queries, key_rows, seg_total, text_len)
    top_score = jnp.max(scores, axis=-1, keepdims=True)
    raised = jnp.exp(scores - top_score)
    totals = jnp.sum(raised, axis=-1, keepdims=True)
    probs_low = (raised / totals).astype(jnp.bfloat16)
    context = jnp.einsum("hqk,hkd->hqd", probs_low, value_rows, preferred_element_type=jnp.float32)
    return context.astype(jnp.bfloat16), top_score + jnp.log(totals)


def attend_backward(text_len, queries, key_rows, value_rows, seg_total, log_total, grad_context):
    scores = score_block(queries, key_rows, seg_total, text_len)
    attn_probs = jnp.exp(scores - log_total)
    grad_probs = jnp.einsum(
        "hqd,hkd->hqk", grad_context, value_rows, preferred_element_type=jnp.float32
    )
    inner_sum = jnp.sum(grad_probs * attn_probs, axis=-1, keepdims=True)
    grad_scores = (attn_probs * (grad_probs - inner_sum)).astype(jnp.bfloat16)
    score_scale = HEAD_DIM ** (-0.5)
    grad_values = jnp.einsum(
        "hqk,hqd->hkd",
        attn_probs.astype(jnp.bfloat16),
        grad_context,
        preferred_element_type=jnp.float32,
    )
    grad_queries = (
        jnp.einsum("hqk,hkd->hqd", grad_scores, key_rows, preferred_element_type=jnp.float32)
        * score_scale
    )
    grad_keys = (
        jnp.einsum("hqk,hqd->hkd", grad_scores, queries, preferred_element_type=jnp.float32)
        * score_scale
    )
    return (
        grad_queries.astype(jnp.bfloat16),
        grad_keys.astype(jnp.bfloat16),
        grad_values.astype(jnp.bfloat16),
    )


def flip_perm(size, bit):
    return [(at, at ^ bit) for at in range(size)]


def body(
    tokens,
    seg_index,
    seg_count,
    weight_query,
    weight_key,
    weight_value,
    weight_out,
    weight_up,
    weight_down,
    bias_query,
    bias_value,
    bias_out,
    bias_up,
    bias_down,
    gain_one,
    shift_one,
    gain_two,
    shift_two,
    cotangent,
):
    low, full = jnp.bfloat16, jnp.float32
    width = tokens.shape[1]
    text_len = seg_index.shape[1]
    seq_len = tokens.shape[0] // seg_count.shape[0]
    slot_total = seq_len - text_len
    half = seq_len // 2
    docs_size = lax.axis_size("docs")
    stages = docs_size.bit_length() - 1
    docs_pos = lax.axis_index("docs")
    heads_pos = lax.axis_index("heads")
    core = heads_pos % 2
    side = heads_pos // 2
    slab = weight_query.shape[1]
    block = weight_query.shape[0]
    hidden = weight_up.shape[1]

    def swap_core(array):
        return lax.ppermute(array, "heads", flip_perm(4, 1))

    def swap_side(array):
        return lax.ppermute(array, "heads", flip_perm(4, 2))

    def swap_docs(array, stage):
        return lax.ppermute(array, "docs", flip_perm(docs_size, 1 << stage))

    def docs_bit(stage):
        return (docs_pos >> stage) & 1

    def join(own, got, bit, axis):
        return jnp.stack([jnp.where(bit == 0, own, got), jnp.where(bit == 0, got, own)], axis)

    def gather_far(shard):
        out = shard
        for step, stage in enumerate(range(stages - 1, 0, -1)):
            out = join(out, swap_docs(out, stage), docs_bit(stage), step)
        return out.reshape((docs_size // 2,) + shard.shape)

    def gather_near(part):
        return join(part, swap_docs(part, 0), docs_bit(0), 1).reshape(
            (docs_size,) + part.shape[1:]
        )

    def gather_side(part):
        return join(part, swap_side(part), side, 0)

    shard_attn = jnp.concatenate(
        [weight_query, weight_key, weight_value, weight_out.T], axis=1
    ).astype(low)
    shard_ffn = jnp.concatenate([weight_up, weight_down.T], axis=1).astype(low)
    far_attn = gather_far(shard_attn)
    shard_ffn, far_attn = lax.optimization_barrier((shard_ffn, far_attn))
    far_ffn = gather_far(shard_ffn)
    pair = 2 * slab
    qk_full = gather_side(gather_near(far_attn[..., :pair])).reshape(2, width, pair)
    vo_side = gather_side(far_attn[..., pair:])
    vo_full = join(vo_side, swap_docs(vo_side, 0), docs_bit(0), 2).reshape(2, width, pair)
    up_full = gather_side(gather_near(far_ffn[..., :hidden])).reshape(2, width, hidden)
    down_side = gather_side(far_ffn[..., hidden:])
    down_full = join(down_side, swap_docs(down_side, 0), docs_bit(0), 2).reshape(2, width, hidden)

    bias_sides = jnp.concatenate([bias_query, bias_value, bias_up])
    bias_sides = join(bias_sides, swap_side(bias_sides), side, 0)
    query_bias = bias_sides[:, :slab]
    value_bias = bias_sides[:, slab:pair]
    hidden_bias = bias_sides[:, pair:]

    doc = lax.dynamic_index_in_dim(tokens.reshape(2, seq_len, width), side, 0, keepdims=False)
    doc_index = lax.dynamic_index_in_dim(seg_index, side, 0, keepdims=False)
    doc_count = lax.dynamic_index_in_dim(seg_count, side, 0, keepdims=False)
    row_start = core * half

    def my_rows(array):
        return lax.dynamic_slice_in_dim(array, row_start, half, 0)

    def reduce_core(part):
        theirs = lax.dynamic_slice_in_dim(part, (1 - core) * half, half, 0).astype(low)
        return my_rows(part) + swap_core(theirs).astype(full)

    def gather_core(rows):
        return join(rows, swap_core(rows), core, 0).reshape(seq_len, width)

    slot_ids = jnp.arange(slot_total, dtype=jnp.int32)
    onehot = (doc_index[:, None] == slot_ids[None, :]).astype(low)
    members = jnp.sum(onehot.astype(full), axis=0)
    divisor = jnp.maximum(members, 1.0)[:, None]
    text_rows = doc[:text_len]
    pooled = contract_rows(onehot, text_rows) / divisor
    slot_live = (slot_ids < doc_count).astype(full)[:, None]
    slot_rows = slot_live * (doc[text_len:].astype(full) + pooled)
    inputs = jnp.concatenate([text_rows.astype(full), slot_rows], axis=0)
    hidden_in = inputs.astype(low)

    def project(weight, bias):
        out = jnp.einsum("rd,sde->sre", hidden_in, weight, preferred_element_type=full)
        return out + bias[:, None, :]

    qk_rows = project(
        qk_full, jnp.concatenate([query_bias, jnp.zeros_like(query_bias)], axis=1)
    ).astype(low)
    v_rows = project(vo_full[..., :slab], value_bias).astype(low)
    out_full = vo_full[..., slab:]
    heads_slab = slab // HEAD_DIM

    def to_heads(array):
        return (
            array.reshape(2, seq_len, heads_slab, HEAD_DIM)
            .transpose(0, 2, 1, 3)
            .reshape(2 * heads_slab, seq_len, HEAD_DIM)
        )

    def from_heads(array):
        return (
            array.reshape(2, heads_slab, seq_len, HEAD_DIM)
            .transpose(0, 2, 1, 3)
            .reshape(2, seq_len, slab)
        )

    query_heads = to_heads(qk_rows[..., :slab])
    key_heads = to_heads(qk_rows[..., slab:])
    value_heads = to_heads(v_rows)
    context_heads, log_total = attend_forward(
        text_len, query_heads, key_heads, value_heads, doc_count
    )
    context = from_heads(context_heads)
    attn_part = jnp.einsum("src,sdc->rd", context, out_full, preferred_element_type=full)
    pre_one = my_rows(inputs) + (reduce_core(attn_part) + bias_out)
    normed_one, scaled_one, inv_one = norm_forward(pre_one, gain_one, shift_one)
    normed_low = gather_core(normed_one.astype(low))
    upward = (
        jnp.einsum("rd,sdh->srh", normed_low, up_full, preferred_element_type=full)
        + hidden_bias[:, None, :]
    )
    activated = jax.nn.gelu(upward, approximate=False).astype(low)
    down_part = jnp.einsum("srh,sdh->rd", activated, down_full, preferred_element_type=full)
    grad_rows_out = lax.dynamic_slice_in_dim(
        cotangent, side * seq_len + row_start, half, 0
    ).astype(full)
    pre_two = normed_one + (reduce_core(down_part) + bias_down)
    normed_two, scaled_two, inv_two = norm_forward(pre_two, gain_two, shift_two)
    layer_out = normed_two.astype(low)
    grad_pre_two = norm_backward(grad_rows_out, scaled_two, inv_two, gain_two)
    gain_two_part = jnp.sum(grad_rows_out * scaled_two, axis=0)
    shift_two_part = jnp.sum(grad_rows_out, axis=0)
    grad_down_half = grad_pre_two.astype(low)
    bias_down_part = jnp.sum(grad_down_half.astype(full), axis=0)
    grad_down_low = gather_core(grad_down_half)
    grad_weight_down = jnp.einsum(
        "rd,srh->sdh", grad_down_low, activated, preferred_element_type=full
    )
    grad_activated = jnp.einsum(
        "rd,sdh->srh", grad_down_low, down_full, preferred_element_type=full
    )
    gelu_value, gelu_back = jax.vjp(partial(jax.nn.gelu, approximate=False), upward)
    grad_up_low = gelu_back(grad_activated)[0].astype(low)
    grad_weight_up = jnp.einsum("rd,srh->sdh", normed_low, grad_up_low, preferred_element_type=full)
    bias_up_part = jnp.sum(grad_up_low.astype(full), axis=1)
    grad_normed_part = jnp.einsum(
        "srh,sdh->rd", grad_up_low, up_full, preferred_element_type=full
    )
    grad_normed = reduce_core(grad_normed_part) + grad_pre_two
    grad_pre_one = norm_backward(grad_normed, scaled_one, inv_one, gain_one)
    gain_one_part = jnp.sum(grad_normed * scaled_one, axis=0)
    shift_one_part = jnp.sum(grad_normed, axis=0)
    grad_branch_half = grad_pre_one.astype(low)
    bias_out_part = jnp.sum(grad_branch_half.astype(full), axis=0)
    grad_branch_low = gather_core(grad_branch_half)
    grad_weight_out = jnp.einsum(
        "rd,src->sdc", grad_branch_low, context, preferred_element_type=full
    )
    grad_context = jnp.einsum(
        "rd,sdc->src", grad_branch_low, out_full, preferred_element_type=full
    ).astype(low)
    grad_q_heads, grad_k_heads, grad_v_heads = attend_backward(
        text_len,
        query_heads,
        key_heads,
        value_heads,
        doc_count,
        log_total,
        to_heads(grad_context),
    )
    grad_qk = jnp.concatenate([from_heads(grad_q_heads), from_heads(grad_k_heads)], axis=2)
    grad_v = from_heads(grad_v_heads)
    grad_weight_qk = jnp.einsum("rd,src->sdc", hidden_in, grad_qk, preferred_element_type=full)
    grad_weight_v = jnp.einsum("rd,src->sdc", hidden_in, grad_v, preferred_element_type=full)
    bias_query_part = jnp.sum(grad_qk[..., :slab].astype(full), axis=1)
    bias_value_part = jnp.sum(grad_v.astype(full), axis=1)
    grad_hidden_part = jnp.einsum(
        "src,sdc->rd", grad_qk, qk_full, preferred_element_type=full
    ) + jnp.einsum("src,sdc->rd", grad_v, vo_full[..., :slab], preferred_element_type=full)
    grad_inputs = (reduce_core(grad_hidden_part) + grad_pre_one).astype(low)
    grad_sides = join(grad_inputs, swap_side(grad_inputs), side, 0)
    grad_all = join(grad_sides, swap_core(grad_sides), core, 1).reshape(2, seq_len, width)
    grad_all = lax.optimization_barrier(grad_all).astype(full)
    onehot_both = (seg_index[:, :, None] == slot_ids[None, None, :]).astype(full)
    divisor_both = jnp.maximum(jnp.sum(onehot_both, axis=1), 1.0)[:, :, None]
    live_both = (slot_ids[None, :] < seg_count[:, None]).astype(full)[:, :, None]
    grad_slots = live_both * grad_all[:, text_len:]
    spread_back = jnp.einsum(
        "gts,gsd->gtd",
        onehot_both,
        grad_slots / divisor_both,
        precision=lax.Precision.HIGHEST,
        preferred_element_type=full,
    )
    grad_tokens = (
        jnp.concatenate([grad_all[:, :text_len] + spread_back, grad_slots], axis=1)
        .reshape(2 * seq_len, width)
        .astype(low)
    )

    def scatter_side(parts):
        theirs = lax.dynamic_index_in_dim(parts, 1 - side, 0, keepdims=False).astype(low)
        mine = lax.dynamic_index_in_dim(parts, side, 0, keepdims=False)
        return mine + swap_side(theirs).astype(full)

    def scatter_docs(parts, stage, axis):
        bit = docs_bit(stage)
        theirs = lax.dynamic_index_in_dim(parts, 1 - bit, axis, keepdims=False).astype(low)
        mine = lax.dynamic_index_in_dim(parts, bit, axis, keepdims=False)
        return mine + swap_docs(theirs, stage).astype(full)

    def scatter_far(parts):
        out = parts.reshape((2,) * (stages - 1) + parts.shape[1:])
        for stage in range(1, stages):
            out = scatter_docs(out, stage, stages - 1 - stage)
        return out

    def scatter_weights(first, second):
        cut = (2, docs_size // 2, 2, block, first.shape[-1])
        first = scatter_side(scatter_docs(first.reshape(cut), 0, 2))
        second = scatter_docs(scatter_side(second.reshape(cut)), 0, 1)
        return scatter_far(jnp.concatenate([first, second], axis=-1))

    total_ffn = scatter_weights(grad_weight_up, grad_weight_down)
    total_attn = scatter_weights(
        grad_weight_qk, jnp.concatenate([grad_weight_v, grad_weight_out], axis=-1)
    )

    def widen(part_sides):
        wide = jnp.zeros((2, 2, part_sides.shape[1]), full)
        return lax.dynamic_update_slice(wide, part_sides[:, None, :], (0, core, 0)).reshape(-1)

    (
        wide_query,
        wide_value,
        wide_up,
        gradient_bias_out,
        gradient_bias_down,
        gradient_gain_one,
        gradient_shift_one,
        gradient_gain_two,
        gradient_shift_two,
    ) = lax.psum(
        (
            widen(bias_query_part),
            widen(bias_value_part),
            widen(bias_up_part),
            bias_out_part,
            bias_down_part,
            gain_one_part,
            shift_one_part,
            gain_two_part,
            shift_two_part,
        ),
        ("docs", "heads"),
    )

    def own_share(wide, size):
        return lax.dynamic_slice_in_dim(wide, heads_pos * size, size, 0)

    return (
        layer_out,
        grad_tokens,
        total_attn[:, :slab],
        total_attn[:, slab:pair],
        total_attn[:, pair : pair + slab],
        total_attn[:, pair + slab :].T,
        total_ffn[:, :hidden],
        total_ffn[:, hidden:].T,
        own_share(wide_query, slab),
        own_share(wide_value, slab),
        gradient_bias_out,
        own_share(wide_up, hidden),
        gradient_bias_down,
        gradient_gain_one,
        gradient_shift_one,
        gradient_gain_two,
        gradient_shift_two,
    )


def solution(mesh):
    placed = (
        P("docs", None),
        P("docs", None),
        P("docs"),
        P("docs", "heads"),
        P("docs", "heads"),
        P("docs", "heads"),
        P("heads", "docs"),
        P("docs", "heads"),
        P("heads", "docs"),
        P("heads"),
        P("heads"),
        P(),
        P("heads"),
        P(),
        P(),
        P(),
        P(),
        P(),
        P("docs", None),
    )
    return jax.shard_map(
        body,
        mesh=mesh,
        in_specs=placed,
        out_specs=(
            P(("docs", "heads"), None),
            P("docs", None),
            P("docs", "heads"),
            P("docs", "heads"),
            P("docs", "heads"),
            P("heads", "docs"),
            P("docs", "heads"),
            P("heads", "docs"),
            P("heads"),
            P("heads"),
            P(),
            P("heads"),
            P(),
            P(),
            P(),
            P(),
            P(),
        ),
        check_vma=False,
    )
```

```python
from functools import partial

import jax
import jax.numpy as jnp
from jax import lax
from jax.experimental import pallas as pl
from jax.experimental.pallas import tpu as pltpu
from jax.sharding import PartitionSpec as P

HEAD_DIM = 64
epsilon = 1e-05
masked_score = -1000000000.0


def norm_forward(pre_rows, gain_vec, shift_vec):
    average = jnp.mean(pre_rows, axis=-1, keepdims=True)
    centered = pre_rows - average
    variance = jnp.mean(centered * centered, axis=-1, keepdims=True)
    inv_std = lax.rsqrt(variance + epsilon)
    scaled = centered * inv_std
    return (scaled * gain_vec + shift_vec, scaled, inv_std)


def norm_backward(grad_out, scaled, inv_std, gain_vec):
    grad_scaled = grad_out * gain_vec
    mean_grad = jnp.mean(grad_scaled, axis=-1, keepdims=True)
    mean_along = jnp.mean(grad_scaled * scaled, axis=-1, keepdims=True)
    return inv_std * (grad_scaled - mean_grad - scaled * mean_along)


def contract_rows(left_side, right_side):
    return lax.dot_general(
        left_side, right_side, (((0,), (0,)), ((), ())), preferred_element_type=jnp.float32
    )


def contract_cols(left_side, right_side):
    return lax.dot_general(
        left_side, right_side, (((1,), (1,)), ((), ())), preferred_element_type=jnp.float32
    )


def mm(left, right, dims=((1,), (0,))):
    return lax.dot_general(left, right, (dims, ((), ())), preferred_element_type=jnp.float32)


NT = ((1,), (1,))


def lane_is_low(shape):
    return lax.broadcasted_iota(jnp.int32, shape, 1) < HEAD_DIM


def swap_rows(block):
    return jnp.concatenate([block[HEAD_DIM:], block[:HEAD_DIM]], axis=0)


def masked_scores(keys, queries_t, limit, text_len):
    scores = mm(keys, queries_t)
    slots = scores[text_len:]
    spot = lax.broadcasted_iota(jnp.int32, slots.shape, 0)
    return scores[:text_len], jnp.where(spot < limit, slots, masked_score)


def attend_fwd_kernel(
    count_ref, hid_ref, w1_ref, w2_ref, b1_ref, b2_ref, qk_ref, v_ref, ctx_ref, lse_ref, part_ref,
    *, text_len
):
    low, full = jnp.bfloat16, jnp.float32
    limit = count_ref[0, 0]
    hid = hid_ref[...]
    w1, w2 = w1_ref[0], w2_ref[0]
    qk = (mm(hid, w1) + b1_ref[0]).astype(low)
    v_a = (mm(hid, w2[:, :128]) + b2_ref[0, :, :128]).astype(low)
    v_b = (mm(hid, w2[:, 256:]) + b2_ref[0, :, 128:]).astype(low)
    is_low = lane_is_low(v_a.shape)
    zero = jnp.zeros_like(v_a)
    v_b = jnp.where(is_low, v_b, zero)
    qk_ref[0] = qk
    v_ref[0, :, :128] = v_a
    v_ref[0, :, 128:] = v_b
    scale = HEAD_DIM ** (-0.5)
    q_a_t = (qk[:, :128] * scale).T
    k_a = qk[:, 128:256]
    qk_b = qk[:, 256:]
    q_b_t = swap_rows((qk_b * scale).T)
    v_a_t, v_b_t = v_a.T, v_b.T

    def head(keys, queries_t, values_t):
        text, slots = masked_scores(keys, queries_t, limit, text_len)
        top = jnp.maximum(
            jnp.max(text, axis=0, keepdims=True), jnp.max(slots, axis=0, keepdims=True)
        )
        text, slots = jnp.exp(text - top), jnp.exp(slots - top)
        total = jnp.sum(text, axis=0, keepdims=True) + jnp.sum(slots, axis=0, keepdims=True)
        raised = jnp.concatenate([text.astype(low), slots.astype(low)], axis=0)
        return mm(values_t, raised) / total, top + jnp.log(total)

    ctx_0, lse_0 = head(jnp.where(is_low, k_a, zero), q_a_t, v_a_t[:HEAD_DIM])
    ctx_1, lse_1 = head(jnp.where(is_low, zero, k_a), q_a_t, v_a_t[HEAD_DIM:])
    ctx_2, lse_2 = head(jnp.where(is_low, zero, qk_b), q_b_t, v_b_t[:HEAD_DIM])
    ctx_a = jnp.concatenate([ctx_0, ctx_1], axis=0).T.astype(low)
    ctx_b = jnp.concatenate([jnp.zeros_like(ctx_2), ctx_2], axis=0).T.astype(low)
    ctx_ref[0, :, :128] = ctx_a
    ctx_ref[0, :, 128:] = ctx_b
    lse_ref[0] = jnp.concatenate([lse_0, lse_1, lse_2, jnp.zeros((5,) + lse_0.shape[1:], full)], 0)
    part = mm(ctx_a, w2[:, 128:256], NT) + mm(ctx_b, w2[:, 256:], NT)

    @pl.when(pl.program_id(0) == 0)
    def _():
        part_ref[...] = part

    @pl.when(pl.program_id(0) > 0)
    def _():
        part_ref[...] += part


def attend_bwd_kernel(
    count_ref, hid_ref, gbl_ref, w1_ref, w2_ref, qk_ref, v_ref, ctx_ref, lse_ref,
    gw1_ref, gw2_ref, sum1_ref, sum2_ref, part_ref, hid_t_ref, gbl_t_ref, *, text_len
):
    low, full = jnp.bfloat16, jnp.float32
    limit = count_ref[0, 0]
    hid, gbl = hid_ref[...], gbl_ref[...]

    @pl.when(pl.program_id(0) == 0)
    def _():
        hid_t_ref[...] = hid.T
        gbl_t_ref[...] = gbl.T

    w1, w2 = w1_ref[0], w2_ref[0]
    qk = qk_ref[0]
    v_a, v_b = v_ref[0, :, :128], v_ref[0, :, 128:]
    do_a = mm(gbl, w2[:, 128:256]).astype(low)
    do_b = mm(gbl, w2[:, 256:]).astype(low)
    is_low = lane_is_low(v_a.shape)
    zero = jnp.zeros_like(v_a)
    scale = HEAD_DIM ** (-0.5)
    q_a = qk[:, :128] * scale
    k_a = qk[:, 128:256]
    k_b = qk[:, 256:]
    q_b = k_b * scale
    q_a_t, k_a_t = q_a.T, k_a.T
    k_b_t = k_b.T
    q_b_t = swap_rows(q_b.T)
    do_a_t, do_b_t = do_a.T, swap_rows(do_b.T)
    lse = lse_ref[0]

    def head(at, keys, queries_t, values, do_t, keys_t, do, queries):
        text, slots = masked_scores(keys, queries_t, limit, text_len)
        log_total = lse[at : at + 1]
        probs = jnp.concatenate([jnp.exp(text - log_total), jnp.exp(slots - log_total)], axis=0)
        grad_probs = mm(values, do_t)
        inner = jnp.sum(grad_probs * probs, axis=0, keepdims=True)
        grad_scores = (probs * (grad_probs - inner)).astype(low)
        grad_v = mm(probs.astype(low), do)
        grad_k = mm(grad_scores, queries)
        grad_q_t = mm(keys_t, grad_scores) * scale
        return grad_q_t, grad_k, grad_v

    dq_0, dk_0, dv_0 = head(
        0, jnp.where(is_low, k_a, zero), q_a_t, jnp.where(is_low, v_a, zero), do_a_t,
        k_a_t[:HEAD_DIM], do_a, q_a,
    )
    dq_1, dk_1, dv_1 = head(
        1, jnp.where(is_low, zero, k_a), q_a_t, jnp.where(is_low, zero, v_a), do_a_t,
        k_a_t[HEAD_DIM:], do_a, q_a,
    )
    dq_2, dk_2, dv_2 = head(
        2, jnp.where(is_low, zero, k_b), q_b_t, v_b, do_b_t, k_b_t[HEAD_DIM:], do_b, q_b
    )
    dq_a = jnp.concatenate([dq_0, dq_1], axis=0).T
    dk_a = jnp.where(is_low, dk_0, dk_1)
    dq_b = jnp.concatenate([dq_2, jnp.zeros_like(dq_2)], axis=0).T
    dqk_b = jnp.where(is_low, dq_b, pltpu.roll(dk_2, HEAD_DIM, 1))
    dqk = jnp.concatenate([dq_a, dk_a, dqk_b], axis=1).astype(low)
    dv_a = jnp.where(is_low, dv_0, dv_1).astype(low)
    dv_b = jnp.where(is_low, pltpu.roll(dv_2, HEAD_DIM, 1), 0.0).astype(low)
    sum1_ref[0] = jnp.sum(dqk.astype(full), axis=0, keepdims=True)
    sum2_ref[0, :, :128] = jnp.sum(dv_a.astype(full), axis=0, keepdims=True)
    sum2_ref[0, :, 128:] = jnp.sum(dv_b.astype(full), axis=0, keepdims=True)
    hid_t, gbl_t = hid_t_ref[...], gbl_t_ref[...]
    gw1_ref[0] = mm(hid_t, dqk).astype(low)
    gw2_ref[0, :, :128] = mm(hid_t, dv_a).astype(low)
    gw2_ref[0, :, 128:256] = mm(gbl_t, ctx_ref[0, :, :128]).astype(low)
    gw2_ref[0, :, 256:] = (mm(hid_t, dv_b) + mm(gbl_t, ctx_ref[0, :, 128:])).astype(low)
    part = mm(dqk, w1, NT) + mm(dv_a, w2[:, :128], NT) + mm(dv_b, w2[:, 256:], NT)

    @pl.when(pl.program_id(0) == 0)
    def _():
        part_ref[...] = part

    @pl.when(pl.program_id(0) > 0)
    def _():
        part_ref[...] += part


def ffn_fwd_kernel(rows_ref, up_ref, down_ref, bias_ref, act_ref, slope_ref, part_ref):
    low = jnp.bfloat16
    upward = mm(rows_ref[...], up_ref[0]) + bias_ref[0]
    gate = 0.5 + 0.5 * lax.erf(upward * (0.5**0.5))
    act = (upward * gate).astype(low)
    bell = jnp.exp(-0.5 * upward * upward) * ((0.5 / jnp.pi) ** 0.5)
    slope_ref[...] = (gate + upward * bell).astype(low)
    act_ref[...] = act
    part = mm(act, down_ref[0], NT)

    @pl.when(pl.program_id(0) == 0)
    def _():
        part_ref[...] = part

    @pl.when(pl.program_id(0) > 0)
    def _():
        part_ref[...] += part


def ffn_bwd_kernel(
    rows_ref, gdl_ref, up_ref, down_ref, act_ref, slope_ref,
    gup_ref, gdown_ref, sum_ref, part_ref, rows_t_ref, gdl_t_ref
):
    low, full = jnp.bfloat16, jnp.float32

    @pl.when(pl.program_id(0) == 0)
    def _():
        rows_t_ref[...] = rows_ref[...].T
        gdl_t_ref[...] = gdl_ref[...].T

    grad_act = mm(gdl_ref[...], down_ref[0])
    gul = (grad_act * slope_ref[...].astype(full)).astype(low)
    sum_ref[0] = jnp.sum(gul.astype(full), axis=0, keepdims=True)
    gdown_ref[0] = mm(gdl_t_ref[...], act_ref[...]).astype(low)
    gup_ref[0] = mm(rows_t_ref[...], gul).astype(low)
    part = mm(gul, up_ref[0], NT)

    @pl.when(pl.program_id(0) == 0)
    def _():
        part_ref[...] = part

    @pl.when(pl.program_id(0) > 0)
    def _():
        part_ref[...] += part


def whole(shape):
    return pl.BlockSpec(shape, lambda at: (0,) * len(shape))


def per_side(shape):
    return pl.BlockSpec((1,) + shape, lambda at: (at,) + (0,) * len(shape))


def shaped(shape, kind=jnp.bfloat16):
    return jax.ShapeDtypeStruct(shape, kind)


def attend_fwd(count, hid, w1, w2, b1, b2, text_len):
    rows, width = hid.shape
    pair = w1.shape[-1]
    return pl.pallas_call(
        partial(attend_fwd_kernel, text_len=text_len),
        grid=(2,),
        in_specs=[
            pl.BlockSpec(memory_space=pltpu.SMEM),
            whole((rows, width)),
            per_side((width, pair)),
            per_side((width, pair)),
            per_side((1, pair)),
            per_side((1, 256)),
        ],
        out_specs=[
            per_side((rows, pair)),
            per_side((rows, 256)),
            per_side((rows, 256)),
            per_side((8, rows)),
            whole((rows, width)),
        ],
        out_shape=[
            shaped((2, rows, pair)),
            shaped((2, rows, 256)),
            shaped((2, rows, 256)),
            shaped((2, 8, rows), jnp.float32),
            shaped((rows, width), jnp.float32),
        ],
        name="attend_fwd",
    )(count, hid, w1, w2, b1, b2)


def attend_bwd(count, hid, gbl, w1, w2, qk, v, ctx, lse, text_len):
    rows, width = hid.shape
    pair = w1.shape[-1]
    return pl.pallas_call(
        partial(attend_bwd_kernel, text_len=text_len),
        grid=(2,),
        in_specs=[
            pl.BlockSpec(memory_space=pltpu.SMEM),
            whole((rows, width)),
            whole((rows, width)),
            per_side((width, pair)),
            per_side((width, pair)),
            per_side((rows, pair)),
            per_side((rows, 256)),
            per_side((rows, 256)),
            per_side((8, rows)),
        ],
        out_specs=[
            per_side((width, pair)),
            per_side((width, pair)),
            per_side((1, pair)),
            per_side((1, 256)),
            whole((rows, width)),
        ],
        out_shape=[
            shaped((2, width, pair)),
            shaped((2, width, pair)),
            shaped((2, 1, pair), jnp.float32),
            shaped((2, 1, 256), jnp.float32),
            shaped((rows, width), jnp.float32),
        ],
        scratch_shapes=[pltpu.VMEM((width, rows), jnp.bfloat16)] * 2,
        name="attend_bwd",
    )(count, hid, gbl, w1, w2, qk, v, ctx, lse)


FFN_CUT = 384


def ffn_specs(rows, width, hidden):
    per = hidden // FFN_CUT
    weight = pl.BlockSpec((1, width, FFN_CUT), lambda at: (at // per, 0, at % per))
    vector = pl.BlockSpec((1, 1, FFN_CUT), lambda at: (at // per, 0, at % per))
    wide = pl.BlockSpec((rows, FFN_CUT), lambda at: (0, at))
    return 2 * per, weight, vector, wide


def ffn_fwd(rows_low, up, down, bias):
    rows, width = rows_low.shape
    hidden = up.shape[-1]
    steps, weight, vector, wide = ffn_specs(rows, width, hidden)
    return pl.pallas_call(
        ffn_fwd_kernel,
        grid=(steps,),
        in_specs=[whole((rows, width)), weight, weight, vector],
        out_specs=[wide, wide, whole((rows, width))],
        out_shape=[
            shaped((rows, 2 * hidden)),
            shaped((rows, 2 * hidden)),
            shaped((rows, width), jnp.float32),
        ],
        name="ffn_fwd",
    )(rows_low, up, down, bias)


def ffn_bwd(rows_low, gdl, up, down, act, slope):
    rows, width = rows_low.shape
    hidden = up.shape[-1]
    steps, weight, vector, wide = ffn_specs(rows, width, hidden)
    return pl.pallas_call(
        ffn_bwd_kernel,
        grid=(steps,),
        in_specs=[whole((rows, width)), whole((rows, width)), weight, weight, wide, wide],
        out_specs=[weight, weight, vector, whole((rows, width))],
        out_shape=[
            shaped((2, width, hidden)),
            shaped((2, width, hidden)),
            shaped((2, 1, hidden), jnp.float32),
            shaped((rows, width), jnp.float32),
        ],
        scratch_shapes=[pltpu.VMEM((width, rows), jnp.bfloat16)] * 2,
        name="ffn_bwd",
    )(rows_low, gdl, up, down, act, slope)


def flip_perm(size, bit):
    return [(at, at ^ bit) for at in range(size)]


def pack(first, second):
    return jnp.concatenate(
        [first[..., :128], second[..., :128], first[..., 128:], second[..., 128:]], axis=-1
    )


def unpack(packed):
    cut = 256 + (packed.shape[-1] - 256) // 2
    return (
        jnp.concatenate([packed[..., :128], packed[..., 256:cut]], axis=-1),
        jnp.concatenate([packed[..., 128:256], packed[..., cut:]], axis=-1),
    )


def body(
    tokens,
    seg_index,
    seg_count,
    weight_query,
    weight_key,
    weight_value,
    weight_out,
    weight_up,
    weight_down,
    bias_query,
    bias_value,
    bias_out,
    bias_up,
    bias_down,
    gain_one,
    shift_one,
    gain_two,
    shift_two,
    cotangent,
):
    low, full = jnp.bfloat16, jnp.float32
    width = tokens.shape[1]
    text_len = seg_index.shape[1]
    seq_len = tokens.shape[0] // seg_count.shape[0]
    slot_total = seq_len - text_len
    half = seq_len // 2
    docs_size = lax.axis_size("docs")
    stages = docs_size.bit_length() - 1
    docs_pos = lax.axis_index("docs")
    heads_pos = lax.axis_index("heads")
    core = heads_pos % 2
    side = heads_pos // 2
    slab = weight_query.shape[1]
    pair = 2 * slab
    block = weight_query.shape[0]
    hidden = weight_up.shape[1]

    def swap_core(array):
        return lax.ppermute(array, "heads", flip_perm(4, 1))

    def swap_side(array):
        return lax.ppermute(array, "heads", flip_perm(4, 2))

    def swap_docs(array, stage):
        return lax.ppermute(array, "docs", flip_perm(docs_size, 1 << stage))

    def docs_bit(stage):
        return (docs_pos >> stage) & 1

    def join(own, got, bit, axis):
        return jnp.stack([jnp.where(bit == 0, own, got), jnp.where(bit == 0, got, own)], axis)

    def gather_far(shard):
        out = shard
        for step, stage in enumerate(range(stages - 1, 0, -1)):
            out = join(out, swap_docs(out, stage), docs_bit(stage), step)
        return out.reshape((docs_size // 2,) + shard.shape)

    def gather_near(part):
        return join(part, swap_docs(part, 0), docs_bit(0), 1).reshape(
            (docs_size,) + part.shape[1:]
        )

    def gather_side(part):
        return join(part, swap_side(part), side, 0)

    shard_attn = jnp.concatenate(
        [pack(weight_query, weight_key), pack(weight_value, weight_out.T)], axis=1
    ).astype(low)
    shard_ffn = jnp.concatenate([weight_up, weight_down.T], axis=1).astype(low)
    far_attn = gather_far(shard_attn)
    shard_ffn, far_attn = lax.optimization_barrier((shard_ffn, far_attn))
    far_ffn = gather_far(shard_ffn)
    qk_full = gather_side(gather_near(far_attn[..., :pair])).reshape(2, width, pair)
    vo_side = gather_side(far_attn[..., pair:])
    vo_full = join(vo_side, swap_docs(vo_side, 0), docs_bit(0), 2).reshape(2, width, pair)
    up_full = gather_side(gather_near(far_ffn[..., :hidden])).reshape(2, width, hidden)
    down_side = gather_side(far_ffn[..., hidden:])
    down_full = join(down_side, swap_docs(down_side, 0), docs_bit(0), 2).reshape(2, width, hidden)

    bias_sides = jnp.concatenate(
        [
            pack(bias_query, jnp.zeros_like(bias_query)),
            bias_value,
            jnp.zeros((256 - slab,), full),
            bias_up,
        ]
    )
    bias_sides = join(bias_sides, swap_side(bias_sides), side, 0)[:, None, :]
    qk_bias = bias_sides[..., :pair]
    v_bias = bias_sides[..., pair : pair + 256]
    hidden_bias = bias_sides[..., pair + 256 :]

    doc = lax.dynamic_index_in_dim(tokens.reshape(2, seq_len, width), side, 0, keepdims=False)
    doc_index = lax.dynamic_index_in_dim(seg_index, side, 0, keepdims=False)
    doc_count = lax.dynamic_index_in_dim(seg_count, side, 0, keepdims=False)
    count_cell = doc_count.reshape(1, 1)
    row_start = core * half

    def my_rows(array):
        return lax.dynamic_slice_in_dim(array, row_start, half, 0)

    def reduce_core(part):
        theirs = lax.dynamic_slice_in_dim(part, (1 - core) * half, half, 0).astype(low)
        return my_rows(part) + swap_core(theirs).astype(full)

    def gather_core(rows):
        return join(rows, swap_core(rows), core, 0).reshape(seq_len, width)

    slot_ids = jnp.arange(slot_total, dtype=jnp.int32)
    onehot = (doc_index[:, None] == slot_ids[None, :]).astype(low)
    members = jnp.sum(onehot.astype(full), axis=0)
    divisor = jnp.maximum(members, 1.0)[:, None]
    text_rows = doc[:text_len]
    pooled = contract_rows(onehot, text_rows) / divisor
    slot_live = (slot_ids < doc_count).astype(full)[:, None]
    slot_rows = slot_live * (doc[text_len:].astype(full) + pooled)
    inputs = jnp.concatenate([text_rows.astype(full), slot_rows], axis=0)
    hidden_in = inputs.astype(low)

    qk_rows, v_rows, context, log_total, attn_part = attend_fwd(
        count_cell, hidden_in, qk_full, vo_full, qk_bias, v_bias, text_len
    )
    pre_one = my_rows(inputs) + (reduce_core(attn_part) + bias_out)
    normed_one, scaled_one, inv_one = norm_forward(pre_one, gain_one, shift_one)
    normed_low = gather_core(normed_one.astype(low))
    activated, slope, down_part = ffn_fwd(normed_low, up_full, down_full, hidden_bias)
    grad_rows_out = lax.dynamic_slice_in_dim(
        cotangent, side * seq_len + row_start, half, 0
    ).astype(full)
    pre_two = normed_one + (reduce_core(down_part) + bias_down)
    normed_two, scaled_two, inv_two = norm_forward(pre_two, gain_two, shift_two)
    layer_out = normed_two.astype(low)
    grad_pre_two = norm_backward(grad_rows_out, scaled_two, inv_two, gain_two)
    gain_two_part = jnp.sum(grad_rows_out * scaled_two, axis=0)
    shift_two_part = jnp.sum(grad_rows_out, axis=0)
    grad_down_half = grad_pre_two.astype(low)
    bias_down_part = jnp.sum(grad_down_half.astype(full), axis=0)
    grad_down_low = gather_core(grad_down_half)
    grad_weight_up, grad_weight_down, bias_up_part, grad_normed_part = ffn_bwd(
        normed_low, grad_down_low, up_full, down_full, activated, slope
    )
    grad_normed = reduce_core(grad_normed_part) + grad_pre_two
    grad_pre_one = norm_backward(grad_normed, scaled_one, inv_one, gain_one)
    gain_one_part = jnp.sum(grad_normed * scaled_one, axis=0)
    shift_one_part = jnp.sum(grad_normed, axis=0)
    grad_branch_half = grad_pre_one.astype(low)
    bias_out_part = jnp.sum(grad_branch_half.astype(full), axis=0)
    grad_branch_low = gather_core(grad_branch_half)
    grad_weight_qk, grad_weight_vo, bias_qk_part, bias_v_part, grad_hidden_part = attend_bwd(
        count_cell,
        hidden_in,
        grad_branch_low,
        qk_full,
        vo_full,
        qk_rows,
        v_rows,
        context,
        log_total,
        text_len,
    )
    grad_inputs = (reduce_core(grad_hidden_part) + grad_pre_one).astype(low)
    grad_sides = join(grad_inputs, swap_side(grad_inputs), side, 0)
    grad_all = join(grad_sides, swap_core(grad_sides), core, 1).reshape(2, seq_len, width)
    grad_all = lax.optimization_barrier(grad_all).astype(full)
    onehot_both = (seg_index[:, :, None] == slot_ids[None, None, :]).astype(full)
    divisor_both = jnp.maximum(jnp.sum(onehot_both, axis=1), 1.0)[:, :, None]
    live_both = (slot_ids[None, :] < seg_count[:, None]).astype(full)[:, :, None]
    grad_slots = live_both * grad_all[:, text_len:]
    spread_back = jnp.einsum(
        "gts,gsd->gtd",
        onehot_both,
        grad_slots / divisor_both,
        precision=lax.Precision.HIGHEST,
        preferred_element_type=full,
    )
    grad_tokens = (
        jnp.concatenate([grad_all[:, :text_len] + spread_back, grad_slots], axis=1)
        .reshape(2 * seq_len, width)
        .astype(low)
    )

    def split_docs(parts, stage, axis):
        bit = docs_bit(stage)
        theirs = lax.dynamic_index_in_dim(parts, 1 - bit, axis, keepdims=False).astype(low)
        return lax.dynamic_index_in_dim(parts, bit, axis, keepdims=False), theirs

    def split_side(parts):
        theirs = lax.dynamic_index_in_dim(parts, 1 - side, 0, keepdims=False).astype(low)
        return lax.dynamic_index_in_dim(parts, side, 0, keepdims=False), theirs

    def exchange(pieces, move):
        mine, theirs = pieces
        return mine.astype(full) + move(theirs).astype(full)

    def exchange_with(pieces, sums, move):
        mine, theirs = pieces
        lanes = theirs.shape[-1]
        sums = sums.reshape(-1, lanes).astype(low)
        flat = theirs.reshape(-1, lanes)
        got = move(jnp.concatenate([flat, sums], axis=0))
        cut = flat.shape[0]
        return (
            mine.astype(full) + got[:cut].reshape(mine.shape).astype(full),
            sums.astype(full) + got[cut:].astype(full),
        )

    def far_axis(stage):
        return stages - 1 - stage

    near_cut = (2, docs_size // 2, 2, block)
    far_cut = (2,) * (stages - 1) + (block,)

    up_parts = grad_weight_up.reshape(near_cut + (hidden,))
    down_parts = grad_weight_down.reshape(near_cut + (hidden,))
    up_parts = exchange(split_docs(up_parts, 0, 2), lambda send: swap_docs(send, 0))
    down_parts = exchange(split_side(down_parts), swap_side)
    up_parts = exchange(split_side(up_parts), swap_side)
    down_parts = exchange(split_docs(down_parts, 0, 1), lambda send: swap_docs(send, 0))
    total_ffn = jnp.concatenate([up_parts, down_parts], axis=-1).reshape(far_cut + (2 * hidden,))
    for stage in range(1, stages):
        total_ffn = exchange(
            split_docs(total_ffn, stage, far_axis(stage)), lambda send: swap_docs(send, stage)
        )

    sums = jnp.concatenate(
        [
            bias_qk_part.reshape(-1),
            bias_v_part.reshape(-1),
            bias_up_part.reshape(-1),
            bias_out_part,
            bias_down_part,
            gain_one_part,
            shift_one_part,
            gain_two_part,
            shift_two_part,
        ]
    )
    used = sums.shape[0]
    sums = jnp.concatenate([sums, jnp.zeros((-used % (16 * pair),), full)])
    qk_parts = grad_weight_qk.reshape(near_cut + (pair,))
    vo_parts = grad_weight_vo.reshape(near_cut + (pair,))
    qk_parts, sums = exchange_with(
        split_docs(qk_parts, 0, 2), sums, lambda send: swap_docs(send, 0)
    )
    vo_parts = exchange(split_side(vo_parts), swap_side)
    qk_parts, sums = exchange_with(split_side(qk_parts), sums, swap_side)
    vo_parts = exchange(split_docs(vo_parts, 0, 1), lambda send: swap_docs(send, 0))
    total_attn = jnp.concatenate([qk_parts, vo_parts], axis=-1).reshape(far_cut + (2 * pair,))
    for stage in range(1, stages):
        total_attn, sums = exchange_with(
            split_docs(total_attn, stage, far_axis(stage)),
            sums,
            lambda send: swap_docs(send, stage),
        )
    sums = sums.reshape(-1)
    ends = [2 * pair, 2 * pair + 512, 2 * pair + 512 + 2 * hidden]
    shared = sums[ends[2] : used]
    shared = (shared + swap_core(shared)).reshape(-1, width)

    def own_side(vector):
        return lax.dynamic_index_in_dim(vector.reshape(2, -1), side, 0, keepdims=False)

    gradient_query, gradient_key = unpack(total_attn[:, :pair])
    gradient_value, gradient_out = unpack(total_attn[:, pair:])
    return (
        layer_out,
        grad_tokens,
        gradient_query,
        gradient_key,
        gradient_value,
        gradient_out.T,
        total_ffn[:, :hidden],
        total_ffn[:, hidden:].T,
        unpack(own_side(sums[: ends[0]]))[0],
        own_side(sums[ends[0] : ends[1]])[:slab],
        shared[0],
        own_side(sums[ends[1] : ends[2]]),
        shared[1],
        shared[2],
        shared[3],
        shared[4],
        shared[5],
    )


def solution(mesh):
    placed = (
        P("docs", None),
        P("docs", None),
        P("docs"),
        P("docs", "heads"),
        P("docs", "heads"),
        P("docs", "heads"),
        P("heads", "docs"),
        P("docs", "heads"),
        P("heads", "docs"),
        P("heads"),
        P("heads"),
        P(),
        P("heads"),
        P(),
        P(),
        P(),
        P(),
        P(),
        P("docs", None),
    )
    return jax.shard_map(
        body,
        mesh=mesh,
        in_specs=placed,
        out_specs=(
            P(("docs", "heads"), None),
            P("docs", None),
            P("docs", "heads"),
            P("docs", "heads"),
            P("docs", "heads"),
            P("heads", "docs"),
            P("docs", "heads"),
            P("heads", "docs"),
            P("heads"),
            P("heads"),
            P(),
            P("heads"),
            P(),
            P(),
            P(),
            P(),
            P(),
        ),
        check_vma=False,
    )
```

```python
from functools import partial

import jax
import jax.numpy as jnp
from jax import lax
from jax.experimental import pallas as pl
from jax.experimental.pallas import tpu as pltpu
from jax.sharding import PartitionSpec as P

HEAD_DIM = 64
epsilon = 1e-05
masked_score = -1000000000.0


def norm_forward(pre_rows, gain_vec, shift_vec):
    average = jnp.mean(pre_rows, axis=-1, keepdims=True)
    centered = pre_rows - average
    variance = jnp.mean(centered * centered, axis=-1, keepdims=True)
    inv_std = lax.rsqrt(variance + epsilon)
    scaled = centered * inv_std
    return (scaled * gain_vec + shift_vec, scaled, inv_std)


def norm_backward(grad_out, scaled, inv_std, gain_vec):
    grad_scaled = grad_out * gain_vec
    mean_grad = jnp.mean(grad_scaled, axis=-1, keepdims=True)
    mean_along = jnp.mean(grad_scaled * scaled, axis=-1, keepdims=True)
    return inv_std * (grad_scaled - mean_grad - scaled * mean_along)


def contract_rows(left_side, right_side):
    return lax.dot_general(
        left_side, right_side, (((0,), (0,)), ((), ())), preferred_element_type=jnp.float32
    )


def contract_cols(left_side, right_side):
    return lax.dot_general(
        left_side, right_side, (((1,), (1,)), ((), ())), preferred_element_type=jnp.float32
    )


def mm(left, right, dims=((1,), (0,))):
    return lax.dot_general(left, right, (dims, ((), ())), preferred_element_type=jnp.float32)


NT = ((1,), (1,))
TN = ((0,), (0,))


def lane_is_low(shape):
    return lax.broadcasted_iota(jnp.int32, shape, 1) < HEAD_DIM


def swap_rows(block):
    return jnp.concatenate([block[HEAD_DIM:], block[:HEAD_DIM]], axis=0)


def masked_scores(keys, queries_t, limit, text_len):
    scores = mm(keys, queries_t)
    slots = scores[text_len:]
    spot = lax.broadcasted_iota(jnp.int32, slots.shape, 0)
    return scores[:text_len], jnp.where(spot < limit, slots, masked_score)


def attend_fwd_kernel(
    count_ref, hid_ref, w1_ref, w2_ref, b1_ref, b2_ref, qk_ref, v_ref, ctx_ref, lse_ref, part_ref,
    *, text_len
):
    low, full = jnp.bfloat16, jnp.float32
    limit = count_ref[0, 0]
    hid = hid_ref[...]
    w1, w2 = w1_ref[0], w2_ref[0]
    qk = (mm(hid, w1) + b1_ref[0]).astype(low)
    v_a = (mm(hid, w2[:, :128]) + b2_ref[0, :, :128]).astype(low)
    v_b = (mm(hid, w2[:, 256:]) + b2_ref[0, :, 128:]).astype(low)
    is_low = lane_is_low(v_a.shape)
    zero = jnp.zeros_like(v_a)
    v_b = jnp.where(is_low, v_b, zero)
    qk_ref[0] = qk
    v_ref[0, :, :128] = v_a
    v_ref[0, :, 128:] = v_b
    scale = HEAD_DIM ** (-0.5)
    q_a_t = (qk[:, :128] * scale).T
    k_a = qk[:, 128:256]
    qk_b = qk[:, 256:]
    q_b_t = swap_rows((qk_b * scale).T)
    v_a_t, v_b_t = v_a.T, v_b.T

    def head(keys, queries_t, values_t):
        text, slots = masked_scores(keys, queries_t, limit, text_len)
        top = jnp.maximum(
            jnp.max(text, axis=0, keepdims=True), jnp.max(slots, axis=0, keepdims=True)
        )
        text, slots = jnp.exp(text - top), jnp.exp(slots - top)
        total = jnp.sum(text, axis=0, keepdims=True) + jnp.sum(slots, axis=0, keepdims=True)
        raised = jnp.concatenate([text.astype(low), slots.astype(low)], axis=0)
        return mm(values_t, raised) / total, top + jnp.log(total)

    ctx_0, lse_0 = head(jnp.where(is_low, k_a, zero), q_a_t, v_a_t[:HEAD_DIM])
    ctx_1, lse_1 = head(jnp.where(is_low, zero, k_a), q_a_t, v_a_t[HEAD_DIM:])
    ctx_2, lse_2 = head(jnp.where(is_low, zero, qk_b), q_b_t, v_b_t[:HEAD_DIM])
    ctx_a = jnp.concatenate([ctx_0, ctx_1], axis=0).T.astype(low)
    ctx_b = jnp.concatenate([jnp.zeros_like(ctx_2), ctx_2], axis=0).T.astype(low)
    ctx_ref[0, :, :128] = ctx_a
    ctx_ref[0, :, 128:] = ctx_b
    lse_ref[0] = jnp.concatenate([lse_0, lse_1, lse_2, jnp.zeros((5,) + lse_0.shape[1:], full)], 0)
    part = mm(ctx_a, w2[:, 128:256], NT) + mm(ctx_b, w2[:, 256:], NT)

    @pl.when(pl.program_id(0) == 0)
    def _():
        part_ref[...] = part

    @pl.when(pl.program_id(0) > 0)
    def _():
        part_ref[...] += part


def attend_bwd_kernel(
    count_ref, hid_ref, gbl_ref, w1_ref, w2_ref, qk_ref, v_ref, ctx_ref, lse_ref,
    gw1_ref, gw2_ref, sum1_ref, sum2_ref, part_ref, hid_t_ref, gbl_t_ref, *, text_len
):
    low, full = jnp.bfloat16, jnp.float32
    limit = count_ref[0, 0]
    hid, gbl = hid_ref[...], gbl_ref[...]

    @pl.when(pl.program_id(0) == 0)
    def _():
        hid_t_ref[...] = hid.T
        gbl_t_ref[...] = gbl.T

    w1, w2 = w1_ref[0], w2_ref[0]
    qk = qk_ref[0]
    v_a, v_b = v_ref[0, :, :128], v_ref[0, :, 128:]
    do_a = mm(gbl, w2[:, 128:256]).astype(low)
    do_b = mm(gbl, w2[:, 256:]).astype(low)
    is_low = lane_is_low(v_a.shape)
    zero = jnp.zeros_like(v_a)
    scale = HEAD_DIM ** (-0.5)
    q_a = qk[:, :128] * scale
    k_a = qk[:, 128:256]
    k_b = qk[:, 256:]
    q_b = k_b * scale
    q_a_t, k_a_t = q_a.T, k_a.T
    k_b_t = k_b.T
    q_b_t = swap_rows(q_b.T)
    do_a_t, do_b_t = do_a.T, swap_rows(do_b.T)
    lse = lse_ref[0]

    def head(at, keys, queries_t, values, do_t, keys_t, do, queries):
        text, slots = masked_scores(keys, queries_t, limit, text_len)
        log_total = lse[at : at + 1]
        probs = jnp.concatenate([jnp.exp(text - log_total), jnp.exp(slots - log_total)], axis=0)
        grad_probs = mm(values, do_t)
        inner = jnp.sum(grad_probs * probs, axis=0, keepdims=True)
        grad_scores = (probs * (grad_probs - inner)).astype(low)
        grad_v = mm(probs.astype(low), do)
        grad_k = mm(grad_scores, queries)
        grad_q_t = mm(keys_t, grad_scores) * scale
        return grad_q_t, grad_k, grad_v

    dq_0, dk_0, dv_0 = head(
        0, jnp.where(is_low, k_a, zero), q_a_t, jnp.where(is_low, v_a, zero), do_a_t,
        k_a_t[:HEAD_DIM], do_a, q_a,
    )
    dq_1, dk_1, dv_1 = head(
        1, jnp.where(is_low, zero, k_a), q_a_t, jnp.where(is_low, zero, v_a), do_a_t,
        k_a_t[HEAD_DIM:], do_a, q_a,
    )
    dq_2, dk_2, dv_2 = head(
        2, jnp.where(is_low, zero, k_b), q_b_t, v_b, do_b_t, k_b_t[HEAD_DIM:], do_b, q_b
    )
    dq_a = jnp.concatenate([dq_0, dq_1], axis=0).T
    dk_a = jnp.where(is_low, dk_0, dk_1)
    dq_b = jnp.concatenate([dq_2, jnp.zeros_like(dq_2)], axis=0).T
    dqk_b = jnp.where(is_low, dq_b, pltpu.roll(dk_2, HEAD_DIM, 1))
    dqk = jnp.concatenate([dq_a, dk_a, dqk_b], axis=1).astype(low)
    dv_a = jnp.where(is_low, dv_0, dv_1).astype(low)
    dv_b = jnp.where(is_low, pltpu.roll(dv_2, HEAD_DIM, 1), 0.0).astype(low)
    sum1_ref[0] = jnp.sum(dqk.astype(full), axis=0, keepdims=True)
    sum2_ref[0, :, :128] = jnp.sum(dv_a.astype(full), axis=0, keepdims=True)
    sum2_ref[0, :, 128:] = jnp.sum(dv_b.astype(full), axis=0, keepdims=True)
    hid_t, gbl_t = hid_t_ref[...], gbl_t_ref[...]
    gw1_ref[0] = mm(hid_t, dqk).astype(low)
    gw2_ref[0, :, :128] = mm(hid_t, dv_a).astype(low)
    gw2_ref[0, :, 128:256] = mm(gbl_t, ctx_ref[0, :, :128]).astype(low)
    gw2_ref[0, :, 256:] = (mm(hid_t, dv_b) + mm(gbl_t, ctx_ref[0, :, 128:])).astype(low)
    part = mm(dqk, w1, NT) + mm(dv_a, w2[:, :128], NT) + mm(dv_b, w2[:, 256:], NT)

    @pl.when(pl.program_id(0) == 0)
    def _():
        part_ref[...] = part

    @pl.when(pl.program_id(0) > 0)
    def _():
        part_ref[...] += part


def ffn_fwd_kernel(rows_ref, up_ref, down_ref, bias_ref, act_ref, slope_ref, part_ref):
    low = jnp.bfloat16
    upward = mm(rows_ref[...], up_ref[0]) + bias_ref[0]
    gate = 0.5 + 0.5 * lax.erf(upward * (0.5**0.5))
    act = (upward * gate).astype(low)
    bell = jnp.exp(-0.5 * upward * upward) * ((0.5 / jnp.pi) ** 0.5)
    slope_ref[...] = (gate + upward * bell).astype(low)
    act_ref[...] = act
    part = mm(act, down_ref[0], NT)

    @pl.when(pl.program_id(0) == 0)
    def _():
        part_ref[...] = part

    @pl.when(pl.program_id(0) > 0)
    def _():
        part_ref[...] += part


def ffn_bwd_kernel(
    rows_ref, gdl_ref, up_ref, down_ref, act_ref, slope_ref,
    gup_ref, gdown_ref, sum_ref, part_ref
):
    low, full = jnp.bfloat16, jnp.float32
    grad_act = mm(gdl_ref[...], down_ref[0])
    gul = (grad_act * slope_ref[...].astype(full)).astype(low)
    sum_ref[0] = jnp.sum(gul.astype(full), axis=0, keepdims=True)
    gdown_ref[0] = mm(gdl_ref[...], act_ref[...], TN).astype(low)
    gup_ref[0] = mm(rows_ref[...], gul, TN).astype(low)
    part = mm(gul, up_ref[0], NT)

    @pl.when(pl.program_id(0) == 0)
    def _():
        part_ref[...] = part

    @pl.when(pl.program_id(0) > 0)
    def _():
        part_ref[...] += part


def whole(shape):
    return pl.BlockSpec(shape, lambda at: (0,) * len(shape))


def per_side(shape):
    return pl.BlockSpec((1,) + shape, lambda at: (at,) + (0,) * len(shape))


def shaped(shape, kind=jnp.bfloat16):
    return jax.ShapeDtypeStruct(shape, kind)


def attend_fwd(count, hid, w1, w2, b1, b2, text_len):
    rows, width = hid.shape
    pair = w1.shape[-1]
    return pl.pallas_call(
        partial(attend_fwd_kernel, text_len=text_len),
        grid=(2,),
        in_specs=[
            pl.BlockSpec(memory_space=pltpu.SMEM),
            whole((rows, width)),
            per_side((width, pair)),
            per_side((width, pair)),
            per_side((1, pair)),
            per_side((1, 256)),
        ],
        out_specs=[
            per_side((rows, pair)),
            per_side((rows, 256)),
            per_side((rows, 256)),
            per_side((8, rows)),
            whole((rows, width)),
        ],
        out_shape=[
            shaped((2, rows, pair)),
            shaped((2, rows, 256)),
            shaped((2, rows, 256)),
            shaped((2, 8, rows), jnp.float32),
            shaped((rows, width), jnp.float32),
        ],
        cost_estimate=pl.CostEstimate(flops=2 * rows * (3 * width * 3 * pair + 3 * rows * pair), bytes_accessed=10 * rows * width, transcendentals=3 * rows * rows * 2),
        name="attend_fwd",
    )(count, hid, w1, w2, b1, b2)


def attend_bwd(count, hid, gbl, w1, w2, qk, v, ctx, lse, text_len):
    rows, width = hid.shape
    pair = w1.shape[-1]
    return pl.pallas_call(
        partial(attend_bwd_kernel, text_len=text_len),
        grid=(2,),
        in_specs=[
            pl.BlockSpec(memory_space=pltpu.SMEM),
            whole((rows, width)),
            whole((rows, width)),
            per_side((width, pair)),
            per_side((width, pair)),
            per_side((rows, pair)),
            per_side((rows, 256)),
            per_side((rows, 256)),
            per_side((8, rows)),
        ],
        out_specs=[
            per_side((width, pair)),
            per_side((width, pair)),
            per_side((1, pair)),
            per_side((1, 256)),
            whole((rows, width)),
        ],
        out_shape=[
            shaped((2, width, pair)),
            shaped((2, width, pair)),
            shaped((2, 1, pair), jnp.float32),
            shaped((2, 1, 256), jnp.float32),
            shaped((rows, width), jnp.float32),
        ],
        scratch_shapes=[pltpu.VMEM((width, rows), jnp.bfloat16)] * 2,
        cost_estimate=pl.CostEstimate(flops=2 * rows * (9 * width * pair + 8 * rows * pair), bytes_accessed=16 * rows * width, transcendentals=3 * rows * rows * 2),
        name="attend_bwd",
    )(count, hid, gbl, w1, w2, qk, v, ctx, lse)


FFN_CUT = 384


def ffn_specs(rows, width, hidden, cut=FFN_CUT):
    per = hidden // cut
    weight = pl.BlockSpec((1, width, cut), lambda at: (at // per, 0, at % per))
    vector = pl.BlockSpec((1, 1, cut), lambda at: (at // per, 0, at % per))
    wide = pl.BlockSpec((rows, cut), lambda at: (0, at))
    return 2 * per, weight, vector, wide


def ffn_fwd(rows_low, up, down, bias):
    rows, width = rows_low.shape
    hidden = up.shape[-1]
    steps, weight, vector, wide = ffn_specs(rows, width, hidden)
    return pl.pallas_call(
        ffn_fwd_kernel,
        grid=(steps,),
        in_specs=[whole((rows, width)), weight, weight, vector],
        out_specs=[wide, wide, whole((rows, width))],
        out_shape=[
            shaped((rows, 2 * hidden)),
            shaped((rows, 2 * hidden)),
            shaped((rows, width), jnp.float32),
        ],
        cost_estimate=pl.CostEstimate(flops=8 * rows * width * hidden, bytes_accessed=12 * rows * width, transcendentals=4 * rows * hidden),
        name="ffn_fwd",
    )(rows_low, up, down, bias)


def ffn_bwd(rows_low, gdl, up, down, act, slope):
    rows, width = rows_low.shape
    hidden = up.shape[-1]
    steps, weight, vector, wide = ffn_specs(rows, width, hidden, hidden)
    return pl.pallas_call(
        ffn_bwd_kernel,
        grid=(steps,),
        in_specs=[whole((rows, width)), whole((rows, width)), weight, weight, wide, wide],
        out_specs=[weight, weight, vector, whole((rows, width))],
        out_shape=[
            shaped((2, width, hidden)),
            shaped((2, width, hidden)),
            shaped((2, 1, hidden), jnp.float32),
            shaped((rows, width), jnp.float32),
        ],
        cost_estimate=pl.CostEstimate(flops=16 * rows * width * hidden, bytes_accessed=20 * rows * width, transcendentals=0),
        name="ffn_bwd",
    )(rows_low, gdl, up, down, act, slope)


def flip_perm(size, bit):
    return [(at, at ^ bit) for at in range(size)]


def pack(first, second):
    return jnp.concatenate(
        [first[..., :128], second[..., :128], first[..., 128:], second[..., 128:]], axis=-1
    )


def unpack(packed):
    cut = 256 + (packed.shape[-1] - 256) // 2
    return (
        jnp.concatenate([packed[..., :128], packed[..., 256:cut]], axis=-1),
        jnp.concatenate([packed[..., 128:256], packed[..., cut:]], axis=-1),
    )


def body(
    tokens,
    seg_index,
    seg_count,
    weight_query,
    weight_key,
    weight_value,
    weight_out,
    weight_up,
    weight_down,
    bias_query,
    bias_value,
    bias_out,
    bias_up,
    bias_down,
    gain_one,
    shift_one,
    gain_two,
    shift_two,
    cotangent,
):
    low, full = jnp.bfloat16, jnp.float32
    width = tokens.shape[1]
    text_len = seg_index.shape[1]
    seq_len = tokens.shape[0] // seg_count.shape[0]
    slot_total = seq_len - text_len
    half = seq_len // 2
    docs_size = lax.axis_size("docs")
    stages = docs_size.bit_length() - 1
    docs_pos = lax.axis_index("docs")
    heads_pos = lax.axis_index("heads")
    core = heads_pos % 2
    side = heads_pos // 2
    slab = weight_query.shape[1]
    pair = 2 * slab
    block = weight_query.shape[0]
    hidden = weight_up.shape[1]

    def swap_core(array):
        return lax.ppermute(array, "heads", flip_perm(4, 1))

    def swap_side(array):
        return lax.ppermute(array, "heads", flip_perm(4, 2))

    def swap_docs(array, stage):
        return lax.ppermute(array, "docs", flip_perm(docs_size, 1 << stage))

    def docs_bit(stage):
        return (docs_pos >> stage) & 1

    def join(own, got, bit, axis):
        return jnp.stack([jnp.where(bit == 0, own, got), jnp.where(bit == 0, got, own)], axis)

    def gather_far(shard):
        out = shard
        for step, stage in enumerate(range(stages - 1, 0, -1)):
            out = join(out, swap_docs(out, stage), docs_bit(stage), step)
        return out.reshape((docs_size // 2,) + shard.shape)

    def gather_near(part):
        return join(part, swap_docs(part, 0), docs_bit(0), 1).reshape(
            (docs_size,) + part.shape[1:]
        )

    def gather_side(part):
        return join(part, swap_side(part), side, 0)

    shard_attn = jnp.concatenate(
        [pack(weight_query, weight_key), pack(weight_value, weight_out.T)], axis=1
    ).astype(low)
    shard_ffn = jnp.concatenate([weight_up, weight_down.T], axis=1).astype(low)
    far_attn = gather_far(shard_attn)
    shard_ffn, far_attn = lax.optimization_barrier((shard_ffn, far_attn))
    far_ffn = gather_far(shard_ffn)
    qk_full = gather_side(gather_near(far_attn[..., :pair])).reshape(2, width, pair)
    vo_side = gather_side(far_attn[..., pair:])
    vo_full = join(vo_side, swap_docs(vo_side, 0), docs_bit(0), 2).reshape(2, width, pair)
    far_up, far_down = far_ffn[..., :hidden], far_ffn[..., hidden:]

    bias_sides = jnp.concatenate(
        [
            pack(bias_query, jnp.zeros_like(bias_query)),
            bias_value,
            jnp.zeros((256 - slab,), full),
            bias_up,
        ]
    )
    bias_sides = join(bias_sides, swap_side(bias_sides), side, 0)[:, None, :]
    qk_bias = bias_sides[..., :pair]
    v_bias = bias_sides[..., pair : pair + 256]
    hidden_bias = bias_sides[..., pair + 256 :]

    doc = lax.dynamic_index_in_dim(tokens.reshape(2, seq_len, width), side, 0, keepdims=False)
    doc_index = lax.dynamic_index_in_dim(seg_index, side, 0, keepdims=False)
    doc_count = lax.dynamic_index_in_dim(seg_count, side, 0, keepdims=False)
    count_cell = doc_count.reshape(1, 1)
    row_start = core * half

    def my_rows(array):
        return lax.dynamic_slice_in_dim(array, row_start, half, 0)

    def reduce_core(part):
        theirs = lax.dynamic_slice_in_dim(part, (1 - core) * half, half, 0).astype(low)
        return my_rows(part) + swap_core(theirs).astype(full)

    def gather_core(rows):
        return join(rows, swap_core(rows), core, 0).reshape(seq_len, width)

    slot_ids = jnp.arange(slot_total, dtype=jnp.int32)
    onehot = (doc_index[:, None] == slot_ids[None, :]).astype(low)
    members = jnp.sum(onehot.astype(full), axis=0)
    divisor = jnp.maximum(members, 1.0)[:, None]
    text_rows = doc[:text_len]
    pooled = contract_rows(onehot, text_rows) / divisor
    slot_live = (slot_ids < doc_count).astype(full)[:, None]
    slot_rows = slot_live * (doc[text_len:].astype(full) + pooled)
    inputs = jnp.concatenate([text_rows.astype(full), slot_rows], axis=0)
    hidden_in = inputs.astype(low)
    hidden_in, up_near, down_side = lax.optimization_barrier((hidden_in, far_up, far_down))
    up_near = gather_near(up_near)
    down_side = gather_side(down_side)

    qk_rows, v_rows, context, log_total, attn_part = attend_fwd(
        count_cell, hidden_in, qk_full, vo_full, qk_bias, v_bias, text_len
    )
    attn_part, up_near, down_side = lax.optimization_barrier((attn_part, up_near, down_side))
    up_full = gather_side(up_near).reshape(2, width, hidden)
    down_full = join(down_side, swap_docs(down_side, 0), docs_bit(0), 2).reshape(2, width, hidden)
    pre_one = my_rows(inputs) + (reduce_core(attn_part) + bias_out)
    normed_one, scaled_one, inv_one = norm_forward(pre_one, gain_one, shift_one)
    normed_low = gather_core(normed_one.astype(low))
    activated, slope, down_part = ffn_fwd(normed_low, up_full, down_full, hidden_bias)
    grad_rows_out = lax.dynamic_slice_in_dim(
        cotangent, side * seq_len + row_start, half, 0
    ).astype(full)
    pre_two = normed_one + (reduce_core(down_part) + bias_down)
    normed_two, scaled_two, inv_two = norm_forward(pre_two, gain_two, shift_two)
    layer_out = normed_two.astype(low)
    grad_pre_two = norm_backward(grad_rows_out, scaled_two, inv_two, gain_two)
    gain_two_part = jnp.sum(grad_rows_out * scaled_two, axis=0)
    shift_two_part = jnp.sum(grad_rows_out, axis=0)
    grad_down_half = grad_pre_two.astype(low)
    bias_down_part = jnp.sum(grad_down_half.astype(full), axis=0)
    grad_down_low = gather_core(grad_down_half)
    grad_weight_up, grad_weight_down, bias_up_part, grad_normed_part = ffn_bwd(
        normed_low, grad_down_low, up_full, down_full, activated, slope
    )
    def split_docs(parts, stage, axis):
        bit = docs_bit(stage)
        theirs = lax.dynamic_index_in_dim(parts, 1 - bit, axis, keepdims=False).astype(low)
        return lax.dynamic_index_in_dim(parts, bit, axis, keepdims=False), theirs

    def split_side(parts):
        theirs = lax.dynamic_index_in_dim(parts, 1 - side, 0, keepdims=False).astype(low)
        return lax.dynamic_index_in_dim(parts, side, 0, keepdims=False), theirs

    def exchange(pieces, move):
        mine, theirs = pieces
        return mine.astype(full) + move(theirs).astype(full)

    def exchange_with(pieces, sums, move):
        mine, theirs = pieces
        lanes = theirs.shape[-1]
        sums = sums.reshape(-1, lanes).astype(low)
        flat = theirs.reshape(-1, lanes)
        got = move(jnp.concatenate([flat, sums], axis=0))
        cut = flat.shape[0]
        return (
            mine.astype(full) + got[:cut].reshape(mine.shape).astype(full),
            sums.astype(full) + got[cut:].astype(full),
        )

    def far_axis(stage):
        return stages - 1 - stage

    near_cut = (2, docs_size // 2, 2, block)
    far_cut = (2,) * (stages - 1) + (block,)

    up_mine, up_theirs = split_docs(grad_weight_up.reshape(near_cut + (hidden,)), 0, 2)
    down_mine, down_theirs = split_side(grad_weight_down.reshape(near_cut + (hidden,)))
    grad_normed_part, up_theirs, down_theirs = lax.optimization_barrier(
        (grad_normed_part, up_theirs, down_theirs)
    )
    up_got = swap_docs(up_theirs, 0)
    down_got = swap_side(down_theirs)
    grad_normed = reduce_core(grad_normed_part) + grad_pre_two
    grad_pre_one = norm_backward(grad_normed, scaled_one, inv_one, gain_one)
    gain_one_part = jnp.sum(grad_normed * scaled_one, axis=0)
    shift_one_part = jnp.sum(grad_normed, axis=0)
    grad_branch_half = grad_pre_one.astype(low)
    bias_out_part = jnp.sum(grad_branch_half.astype(full), axis=0)
    grad_branch_low = gather_core(grad_branch_half)
    grad_weight_qk, grad_weight_vo, bias_qk_part, bias_v_part, grad_hidden_part = attend_bwd(
        count_cell,
        hidden_in,
        grad_branch_low,
        qk_full,
        vo_full,
        qk_rows,
        v_rows,
        context,
        log_total,
        text_len,
    )
    grad_inputs = (reduce_core(grad_hidden_part) + grad_pre_one).astype(low)
    grad_sides = join(grad_inputs, swap_side(grad_inputs), side, 0)
    grad_all = join(grad_sides, swap_core(grad_sides), core, 1).reshape(2, seq_len, width)
    grad_all = lax.optimization_barrier(grad_all).astype(full)
    onehot_both = (seg_index[:, :, None] == slot_ids[None, None, :]).astype(full)
    divisor_both = jnp.maximum(jnp.sum(onehot_both, axis=1), 1.0)[:, :, None]
    live_both = (slot_ids[None, :] < seg_count[:, None]).astype(full)[:, :, None]
    grad_slots = live_both * grad_all[:, text_len:]
    spread_back = jnp.einsum(
        "gts,gsd->gtd",
        onehot_both,
        grad_slots / divisor_both,
        precision=lax.Precision.HIGHEST,
        preferred_element_type=full,
    )
    grad_tokens = (
        jnp.concatenate([grad_all[:, :text_len] + spread_back, grad_slots], axis=1)
        .reshape(2 * seq_len, width)
        .astype(low)
    )

    up_parts = up_mine.astype(full) + up_got.astype(full)
    down_parts = down_mine.astype(full) + down_got.astype(full)
    up_parts = exchange(split_side(up_parts), swap_side)
    down_parts = exchange(split_docs(down_parts, 0, 1), lambda send: swap_docs(send, 0))
    total_ffn = jnp.concatenate([up_parts, down_parts], axis=-1).reshape(far_cut + (2 * hidden,))
    for stage in range(1, stages):
        total_ffn = exchange(
            split_docs(total_ffn, stage, far_axis(stage)), lambda send: swap_docs(send, stage)
        )

    sums = jnp.concatenate(
        [
            bias_qk_part.reshape(-1),
            bias_v_part.reshape(-1),
            bias_up_part.reshape(-1),
            bias_out_part,
            bias_down_part,
            gain_one_part,
            shift_one_part,
            gain_two_part,
            shift_two_part,
        ]
    )
    used = sums.shape[0]
    sums = jnp.concatenate([sums, jnp.zeros((-used % (16 * pair),), full)])
    qk_parts = grad_weight_qk.reshape(near_cut + (pair,))
    vo_parts = grad_weight_vo.reshape(near_cut + (pair,))
    qk_parts, sums = exchange_with(
        split_docs(qk_parts, 0, 2), sums, lambda send: swap_docs(send, 0)
    )
    vo_parts = exchange(split_side(vo_parts), swap_side)
    qk_parts, sums = exchange_with(split_side(qk_parts), sums, swap_side)
    vo_parts = exchange(split_docs(vo_parts, 0, 1), lambda send: swap_docs(send, 0))
    total_attn = jnp.concatenate([qk_parts, vo_parts], axis=-1).reshape(far_cut + (2 * pair,))
    for stage in range(1, stages):
        total_attn, sums = exchange_with(
            split_docs(total_attn, stage, far_axis(stage)),
            sums,
            lambda send: swap_docs(send, stage),
        )
    sums = sums.reshape(-1)
    ends = [2 * pair, 2 * pair + 512, 2 * pair + 512 + 2 * hidden]
    shared = sums[ends[2] : used]
    shared = (shared + swap_core(shared)).reshape(-1, width)

    def own_side(vector):
        return lax.dynamic_index_in_dim(vector.reshape(2, -1), side, 0, keepdims=False)

    gradient_query, gradient_key = unpack(total_attn[:, :pair])
    gradient_value, gradient_out = unpack(total_attn[:, pair:])
    return (
        layer_out,
        grad_tokens,
        gradient_query,
        gradient_key,
        gradient_value,
        gradient_out.T,
        total_ffn[:, :hidden],
        total_ffn[:, hidden:].T,
        unpack(own_side(sums[: ends[0]]))[0],
        own_side(sums[ends[0] : ends[1]])[:slab],
        shared[0],
        own_side(sums[ends[1] : ends[2]]),
        shared[1],
        shared[2],
        shared[3],
        shared[4],
        shared[5],
    )


def solution(mesh):
    placed = (
        P("docs", None),
        P("docs", None),
        P("docs"),
        P("docs", "heads"),
        P("docs", "heads"),
        P("docs", "heads"),
        P("heads", "docs"),
        P("docs", "heads"),
        P("heads", "docs"),
        P("heads"),
        P("heads"),
        P(),
        P("heads"),
        P(),
        P(),
        P(),
        P(),
        P(),
        P("docs", None),
    )
    return jax.shard_map(
        body,
        mesh=mesh,
        in_specs=placed,
        out_specs=(
            P(("docs", "heads"), None),
            P("docs", None),
            P("docs", "heads"),
            P("docs", "heads"),
            P("docs", "heads"),
            P("heads", "docs"),
            P("docs", "heads"),
            P("heads", "docs"),
            P("heads"),
            P("heads"),
            P(),
            P("heads"),
            P(),
            P(),
            P(),
            P(),
            P(),
        ),
        check_vma=False,
    )
```

```python
from functools import partial

import jax
import jax.numpy as jnp
from jax import lax
from jax.experimental import pallas as pl
from jax.experimental.pallas import tpu as pltpu
from jax.sharding import PartitionSpec as P

HEAD_DIM = 64
epsilon = 1e-05
masked_score = -1000000000.0


def norm_forward(pre_rows, gain_vec, shift_vec):
    average = jnp.mean(pre_rows, axis=-1, keepdims=True)
    centered = pre_rows - average
    variance = jnp.mean(centered * centered, axis=-1, keepdims=True)
    inv_std = lax.rsqrt(variance + epsilon)
    scaled = centered * inv_std
    return (scaled * gain_vec + shift_vec, scaled, inv_std)


def norm_backward(grad_out, scaled, inv_std, gain_vec):
    grad_scaled = grad_out * gain_vec
    mean_grad = jnp.mean(grad_scaled, axis=-1, keepdims=True)
    mean_along = jnp.mean(grad_scaled * scaled, axis=-1, keepdims=True)
    return inv_std * (grad_scaled - mean_grad - scaled * mean_along)


def contract_rows(left_side, right_side):
    return lax.dot_general(
        left_side, right_side, (((0,), (0,)), ((), ())), preferred_element_type=jnp.float32
    )


def contract_cols(left_side, right_side):
    return lax.dot_general(
        left_side, right_side, (((1,), (1,)), ((), ())), preferred_element_type=jnp.float32
    )


def mm(left, right, dims=((1,), (0,))):
    return lax.dot_general(left, right, (dims, ((), ())), preferred_element_type=jnp.float32)


NT = ((1,), (1,))
TN = ((0,), (0,))


def lane_is_low(shape):
    return lax.broadcasted_iota(jnp.int32, shape, 1) < HEAD_DIM


def swap_rows(block):
    return jnp.concatenate([block[HEAD_DIM:], block[:HEAD_DIM]], axis=0)


def masked_scores(keys, queries_t, limit, text_len):
    scores = mm(keys, queries_t)
    slots = scores[text_len:]
    spot = lax.broadcasted_iota(jnp.int32, slots.shape, 0)
    return scores[:text_len], jnp.where(spot < limit, slots, masked_score)


def attend_fwd_kernel(
    count_ref, hid_ref, w1_ref, w2_ref, b1_ref, b2_ref, qk_ref, v_ref, ctx_ref, lse_ref, part_ref,
    *, text_len
):
    low, full = jnp.bfloat16, jnp.float32
    limit = count_ref[0, 0]
    hid = hid_ref[...]
    w1, w2 = w1_ref[0], w2_ref[0]
    qk = (mm(hid, w1) + b1_ref[0]).astype(low)
    v_a = (mm(hid, w2[:, :128]) + b2_ref[0, :, :128]).astype(low)
    v_b = (mm(hid, w2[:, 256:]) + b2_ref[0, :, 128:]).astype(low)
    is_low = lane_is_low(v_a.shape)
    zero = jnp.zeros_like(v_a)
    v_b = jnp.where(is_low, v_b, zero)
    qk_ref[0] = qk
    v_ref[0, :, :128] = v_a
    v_ref[0, :, 128:] = v_b
    scale = HEAD_DIM ** (-0.5)
    q_a_t = (qk[:, :128] * scale).T
    k_a = qk[:, 128:256]
    qk_b = qk[:, 256:]
    q_b_t = swap_rows((qk_b * scale).T)
    v_a_t, v_b_t = v_a.T, v_b.T

    def head(keys, queries_t, values_t):
        text, slots = masked_scores(keys, queries_t, limit, text_len)
        top = jnp.maximum(
            jnp.max(text, axis=0, keepdims=True), jnp.max(slots, axis=0, keepdims=True)
        )
        text, slots = jnp.exp(text - top), jnp.exp(slots - top)
        total = jnp.sum(text, axis=0, keepdims=True) + jnp.sum(slots, axis=0, keepdims=True)
        raised = jnp.concatenate([text.astype(low), slots.astype(low)], axis=0)
        return mm(values_t, raised) / total, top + jnp.log(total)

    ctx_0, lse_0 = head(jnp.where(is_low, k_a, zero), q_a_t, v_a_t[:HEAD_DIM])
    ctx_1, lse_1 = head(jnp.where(is_low, zero, k_a), q_a_t, v_a_t[HEAD_DIM:])
    ctx_2, lse_2 = head(jnp.where(is_low, zero, qk_b), q_b_t, v_b_t[:HEAD_DIM])
    ctx_a = jnp.concatenate([ctx_0, ctx_1], axis=0).T.astype(low)
    ctx_b = jnp.concatenate([jnp.zeros_like(ctx_2), ctx_2], axis=0).T.astype(low)
    ctx_ref[0, :, :128] = ctx_a
    ctx_ref[0, :, 128:] = ctx_b
    lse_ref[0] = jnp.concatenate([lse_0, lse_1, lse_2, jnp.zeros((5,) + lse_0.shape[1:], full)], 0)
    part = mm(ctx_a, w2[:, 128:256], NT) + mm(ctx_b, w2[:, 256:], NT)

    @pl.when(pl.program_id(0) == 0)
    def _():
        part_ref[...] = part

    @pl.when(pl.program_id(0) > 0)
    def _():
        part_ref[...] += part


def attend_bwd_kernel(
    count_ref, hid_ref, gbl_ref, w1_ref, w2_ref, qk_ref, v_ref, ctx_ref, lse_ref,
    gw1_ref, gw2_ref, sum1_ref, sum2_ref, part_ref, hid_t_ref, gbl_t_ref, *, text_len
):
    low, full = jnp.bfloat16, jnp.float32
    limit = count_ref[0, 0]
    hid, gbl = hid_ref[...], gbl_ref[...]

    @pl.when(pl.program_id(0) == 0)
    def _():
        hid_t_ref[...] = hid.T
        gbl_t_ref[...] = gbl.T

    w1, w2 = w1_ref[0], w2_ref[0]
    qk = qk_ref[0]
    v_a, v_b = v_ref[0, :, :128], v_ref[0, :, 128:]
    do_a = mm(gbl, w2[:, 128:256]).astype(low)
    do_b = mm(gbl, w2[:, 256:]).astype(low)
    is_low = lane_is_low(v_a.shape)
    zero = jnp.zeros_like(v_a)
    scale = HEAD_DIM ** (-0.5)
    q_a = qk[:, :128] * scale
    k_a = qk[:, 128:256]
    k_b = qk[:, 256:]
    q_b = k_b * scale
    q_a_t, k_a_t = q_a.T, k_a.T
    k_b_t = k_b.T
    q_b_t = swap_rows(q_b.T)
    do_a_t, do_b_t = do_a.T, swap_rows(do_b.T)
    lse = lse_ref[0]

    def head(at, keys, queries_t, values, do_t, keys_t, do, queries):
        text, slots = masked_scores(keys, queries_t, limit, text_len)
        log_total = lse[at : at + 1]
        probs = jnp.concatenate([jnp.exp(text - log_total), jnp.exp(slots - log_total)], axis=0)
        grad_probs = mm(values, do_t)
        inner = jnp.sum(grad_probs * probs, axis=0, keepdims=True)
        grad_scores = (probs * (grad_probs - inner)).astype(low)
        grad_v = mm(probs.astype(low), do)
        grad_k = mm(grad_scores, queries)
        grad_q_t = mm(keys_t, grad_scores) * scale
        return grad_q_t, grad_k, grad_v

    dq_0, dk_0, dv_0 = head(
        0, jnp.where(is_low, k_a, zero), q_a_t, jnp.where(is_low, v_a, zero), do_a_t,
        k_a_t[:HEAD_DIM], do_a, q_a,
    )
    dq_1, dk_1, dv_1 = head(
        1, jnp.where(is_low, zero, k_a), q_a_t, jnp.where(is_low, zero, v_a), do_a_t,
        k_a_t[HEAD_DIM:], do_a, q_a,
    )
    dq_2, dk_2, dv_2 = head(
        2, jnp.where(is_low, zero, k_b), q_b_t, v_b, do_b_t, k_b_t[HEAD_DIM:], do_b, q_b
    )
    dq_a = jnp.concatenate([dq_0, dq_1], axis=0).T
    dk_a = jnp.where(is_low, dk_0, dk_1)
    dq_b = jnp.concatenate([dq_2, jnp.zeros_like(dq_2)], axis=0).T
    dqk_b = jnp.where(is_low, dq_b, pltpu.roll(dk_2, HEAD_DIM, 1))
    dqk = jnp.concatenate([dq_a, dk_a, dqk_b], axis=1).astype(low)
    dv_a = jnp.where(is_low, dv_0, dv_1).astype(low)
    dv_b = jnp.where(is_low, pltpu.roll(dv_2, HEAD_DIM, 1), 0.0).astype(low)
    sum1_ref[0] = jnp.sum(dqk.astype(full), axis=0, keepdims=True)
    sum2_ref[0, :, :128] = jnp.sum(dv_a.astype(full), axis=0, keepdims=True)
    sum2_ref[0, :, 128:] = jnp.sum(dv_b.astype(full), axis=0, keepdims=True)
    hid_t, gbl_t = hid_t_ref[...], gbl_t_ref[...]
    gw1_ref[0] = mm(hid_t, dqk).astype(low)
    gw2_ref[0, :, :128] = mm(hid_t, dv_a).astype(low)
    gw2_ref[0, :, 128:256] = mm(gbl_t, ctx_ref[0, :, :128]).astype(low)
    gw2_ref[0, :, 256:] = (mm(hid_t, dv_b) + mm(gbl_t, ctx_ref[0, :, 128:])).astype(low)
    part = mm(dqk, w1, NT) + mm(dv_a, w2[:, :128], NT) + mm(dv_b, w2[:, 256:], NT)

    @pl.when(pl.program_id(0) == 0)
    def _():
        part_ref[...] = part

    @pl.when(pl.program_id(0) > 0)
    def _():
        part_ref[...] += part


def ffn_fwd_kernel(rows_ref, up_ref, down_ref, bias_ref, act_ref, slope_ref, part_ref):
    low = jnp.bfloat16
    upward = mm(rows_ref[...], up_ref[0]) + bias_ref[0]
    gate = 0.5 + 0.5 * lax.erf(upward * (0.5**0.5))
    act = (upward * gate).astype(low)
    bell = jnp.exp(-0.5 * upward * upward) * ((0.5 / jnp.pi) ** 0.5)
    slope_ref[...] = (gate + upward * bell).astype(low)
    act_ref[...] = act
    part = mm(act, down_ref[0], NT)

    @pl.when(pl.program_id(0) == 0)
    def _():
        part_ref[...] = part

    @pl.when(pl.program_id(0) > 0)
    def _():
        part_ref[...] += part


def ffn_bwd_kernel(
    rows_ref, gdl_ref, up_ref, down_ref, act_ref, slope_ref,
    gup_ref, gdown_ref, sum_ref, part_ref
):
    low, full = jnp.bfloat16, jnp.float32
    grad_act = mm(gdl_ref[...], down_ref[0])
    gul = (grad_act * slope_ref[...].astype(full)).astype(low)
    sum_ref[0] = jnp.sum(gul.astype(full), axis=0, keepdims=True)
    gdown_ref[0] = mm(gdl_ref[...], act_ref[...], TN).astype(low)
    gup_ref[0] = mm(rows_ref[...], gul, TN).astype(low)
    part = mm(gul, up_ref[0], NT)

    @pl.when(pl.program_id(0) == 0)
    def _():
        part_ref[...] = part

    @pl.when(pl.program_id(0) > 0)
    def _():
        part_ref[...] += part


def whole(shape):
    return pl.BlockSpec(shape, lambda at: (0,) * len(shape))


def per_side(shape):
    return pl.BlockSpec((1,) + shape, lambda at: (at,) + (0,) * len(shape))


def shaped(shape, kind=jnp.bfloat16):
    return jax.ShapeDtypeStruct(shape, kind)


def attend_fwd(count, hid, w1, w2, b1, b2, text_len):
    rows, width = hid.shape
    pair = w1.shape[-1]
    return pl.pallas_call(
        partial(attend_fwd_kernel, text_len=text_len),
        grid=(2,),
        in_specs=[
            pl.BlockSpec(memory_space=pltpu.SMEM),
            whole((rows, width)),
            per_side((width, pair)),
            per_side((width, pair)),
            per_side((1, pair)),
            per_side((1, 256)),
        ],
        out_specs=[
            per_side((rows, pair)),
            per_side((rows, 256)),
            per_side((rows, 256)),
            per_side((8, rows)),
            whole((rows, width)),
        ],
        out_shape=[
            shaped((2, rows, pair)),
            shaped((2, rows, 256)),
            shaped((2, rows, 256)),
            shaped((2, 8, rows), jnp.float32),
            shaped((rows, width), jnp.float32),
        ],
        cost_estimate=pl.CostEstimate(flops=2 * rows * (3 * width * 3 * pair + 3 * rows * pair), bytes_accessed=10 * rows * width, transcendentals=3 * rows * rows * 2),
        name="attend_fwd",
    )(count, hid, w1, w2, b1, b2)


def attend_bwd(count, hid, gbl, w1, w2, qk, v, ctx, lse, text_len):
    rows, width = hid.shape
    pair = w1.shape[-1]
    return pl.pallas_call(
        partial(attend_bwd_kernel, text_len=text_len),
        grid=(2,),
        in_specs=[
            pl.BlockSpec(memory_space=pltpu.SMEM),
            whole((rows, width)),
            whole((rows, width)),
            per_side((width, pair)),
            per_side((width, pair)),
            per_side((rows, pair)),
            per_side((rows, 256)),
            per_side((rows, 256)),
            per_side((8, rows)),
        ],
        out_specs=[
            per_side((width, pair)),
            per_side((width, pair)),
            per_side((1, pair)),
            per_side((1, 256)),
            whole((rows, width)),
        ],
        out_shape=[
            shaped((2, width, pair)),
            shaped((2, width, pair)),
            shaped((2, 1, pair), jnp.float32),
            shaped((2, 1, 256), jnp.float32),
            shaped((rows, width), jnp.float32),
        ],
        scratch_shapes=[pltpu.VMEM((width, rows), jnp.bfloat16)] * 2,
        cost_estimate=pl.CostEstimate(flops=2 * rows * (9 * width * pair + 8 * rows * pair), bytes_accessed=16 * rows * width, transcendentals=3 * rows * rows * 2),
        name="attend_bwd",
    )(count, hid, gbl, w1, w2, qk, v, ctx, lse)


FFN_CUT = 384


def ffn_specs(rows, width, hidden, cut=FFN_CUT):
    per = hidden // cut
    weight = pl.BlockSpec((1, width, cut), lambda at: (at // per, 0, at % per))
    vector = pl.BlockSpec((1, 1, cut), lambda at: (at // per, 0, at % per))
    wide = pl.BlockSpec((rows, cut), lambda at: (0, at))
    return 2 * per, weight, vector, wide


def ffn_fwd(rows_low, up, down, bias):
    rows, width = rows_low.shape
    hidden = up.shape[-1]
    steps, weight, vector, wide = ffn_specs(rows, width, hidden)
    return pl.pallas_call(
        ffn_fwd_kernel,
        grid=(steps,),
        in_specs=[whole((rows, width)), weight, weight, vector],
        out_specs=[wide, wide, whole((rows, width))],
        out_shape=[
            shaped((rows, 2 * hidden)),
            shaped((rows, 2 * hidden)),
            shaped((rows, width), jnp.float32),
        ],
        cost_estimate=pl.CostEstimate(flops=8 * rows * width * hidden, bytes_accessed=12 * rows * width, transcendentals=4 * rows * hidden),
        name="ffn_fwd",
    )(rows_low, up, down, bias)


def ffn_bwd(rows_low, gdl, up, down, act, slope):
    rows, width = rows_low.shape
    hidden = up.shape[-1]
    steps, weight, vector, wide = ffn_specs(rows, width, hidden, hidden)
    return pl.pallas_call(
        ffn_bwd_kernel,
        grid=(steps,),
        in_specs=[whole((rows, width)), whole((rows, width)), weight, weight, wide, wide],
        out_specs=[weight, weight, vector, whole((rows, width))],
        out_shape=[
            shaped((2, width, hidden)),
            shaped((2, width, hidden)),
            shaped((2, 1, hidden), jnp.float32),
            shaped((rows, width), jnp.float32),
        ],
        cost_estimate=pl.CostEstimate(flops=16 * rows * width * hidden, bytes_accessed=20 * rows * width, transcendentals=0),
        name="ffn_bwd",
    )(rows_low, gdl, up, down, act, slope)


def flip_perm(size, bit):
    return [(at, at ^ bit) for at in range(size)]


def pack(first, second):
    return jnp.concatenate(
        [first[..., :128], second[..., :128], first[..., 128:], second[..., 128:]], axis=-1
    )


def unpack(packed):
    cut = 256 + (packed.shape[-1] - 256) // 2
    return (
        jnp.concatenate([packed[..., :128], packed[..., 256:cut]], axis=-1),
        jnp.concatenate([packed[..., 128:256], packed[..., cut:]], axis=-1),
    )


def body(
    tokens,
    seg_index,
    seg_count,
    weight_query,
    weight_key,
    weight_value,
    weight_out,
    weight_up,
    weight_down,
    bias_query,
    bias_value,
    bias_out,
    bias_up,
    bias_down,
    gain_one,
    shift_one,
    gain_two,
    shift_two,
    cotangent,
):
    low, full = jnp.bfloat16, jnp.float32
    width = tokens.shape[1]
    text_len = seg_index.shape[1]
    seq_len = tokens.shape[0] // seg_count.shape[0]
    slot_total = seq_len - text_len
    half = seq_len // 2
    docs_size = lax.axis_size("docs")
    stages = docs_size.bit_length() - 1
    docs_pos = lax.axis_index("docs")
    heads_pos = lax.axis_index("heads")
    core = heads_pos % 2
    side = heads_pos // 2
    slab = weight_query.shape[1]
    pair = 2 * slab
    block = weight_query.shape[0]
    hidden = weight_up.shape[1]

    def swap_core(array):
        return lax.ppermute(array, "heads", flip_perm(4, 1))

    def swap_side(array):
        return lax.ppermute(array, "heads", flip_perm(4, 2))

    def swap_docs(array, stage):
        return lax.ppermute(array, "docs", flip_perm(docs_size, 1 << stage))

    def docs_bit(stage):
        return (docs_pos >> stage) & 1

    def join(own, got, bit, axis):
        return jnp.stack([jnp.where(bit == 0, own, got), jnp.where(bit == 0, got, own)], axis)

    def gather_far(shard):
        out = shard
        for step, stage in enumerate(range(stages - 1, 0, -1)):
            out = join(out, swap_docs(out, stage), docs_bit(stage), step)
        return out.reshape((docs_size // 2,) + shard.shape)

    def gather_near(part):
        return join(part, swap_docs(part, 0), docs_bit(0), 1).reshape(
            (docs_size,) + part.shape[1:]
        )

    def gather_side(part):
        return join(part, swap_side(part), side, 0)

    shard_attn = jnp.concatenate(
        [pack(weight_query, weight_key), pack(weight_value, weight_out.T)], axis=1
    ).astype(low)
    shard_ffn = jnp.concatenate([weight_up, weight_down.T], axis=1).astype(low)
    far_attn = gather_far(shard_attn)
    shard_ffn, far_attn = lax.optimization_barrier((shard_ffn, far_attn))
    got_ffn = swap_docs(shard_ffn, stages - 1)
    qk_near = gather_near(far_attn[..., :pair])
    vo_side = gather_side(far_attn[..., pair:])
    got_ffn = lax.optimization_barrier((got_ffn, qk_near, vo_side))[0]
    far_ffn = join(shard_ffn, got_ffn, docs_bit(stages - 1), 0)
    for step, stage in enumerate(range(stages - 2, 0, -1)):
        far_ffn = join(far_ffn, swap_docs(far_ffn, stage), docs_bit(stage), step + 1)
    far_ffn = far_ffn.reshape((docs_size // 2,) + shard_ffn.shape)
    qk_full = gather_side(qk_near).reshape(2, width, pair)
    vo_full = join(vo_side, swap_docs(vo_side, 0), docs_bit(0), 2).reshape(2, width, pair)
    far_up, far_down = far_ffn[..., :hidden], far_ffn[..., hidden:]

    bias_sides = jnp.concatenate(
        [
            pack(bias_query, jnp.zeros_like(bias_query)),
            bias_value,
            jnp.zeros((256 - slab,), full),
            bias_up,
        ]
    )
    bias_sides = join(bias_sides, swap_side(bias_sides), side, 0)[:, None, :]
    qk_bias = bias_sides[..., :pair]
    v_bias = bias_sides[..., pair : pair + 256]
    hidden_bias = bias_sides[..., pair + 256 :]

    doc = lax.dynamic_index_in_dim(tokens.reshape(2, seq_len, width), side, 0, keepdims=False)
    doc_index = lax.dynamic_index_in_dim(seg_index, side, 0, keepdims=False)
    doc_count = lax.dynamic_index_in_dim(seg_count, side, 0, keepdims=False)
    count_cell = doc_count.reshape(1, 1)
    row_start = core * half

    def my_rows(array):
        return lax.dynamic_slice_in_dim(array, row_start, half, 0)

    def core_halves(part):
        theirs = lax.dynamic_slice_in_dim(part, (1 - core) * half, half, 0).astype(low)
        return my_rows(part), swap_core(theirs)

    def reduce_core(part):
        mine, got = core_halves(part)
        return mine + got.astype(full)

    def gather_core(rows):
        return join(rows, swap_core(rows), core, 0).reshape(seq_len, width)

    slot_ids = jnp.arange(slot_total, dtype=jnp.int32)
    onehot = (doc_index[:, None] == slot_ids[None, :]).astype(low)
    members = jnp.sum(onehot.astype(full), axis=0)
    divisor = jnp.maximum(members, 1.0)[:, None]
    text_rows = doc[:text_len]
    pooled = contract_rows(onehot, text_rows) / divisor
    slot_live = (slot_ids < doc_count).astype(full)[:, None]
    slot_rows = slot_live * (doc[text_len:].astype(full) + pooled)
    inputs = jnp.concatenate([text_rows.astype(full), slot_rows], axis=0)
    hidden_in = inputs.astype(low)
    hidden_in, up_near, down_side = lax.optimization_barrier((hidden_in, far_up, far_down))
    up_near = gather_near(up_near)
    down_side = gather_side(down_side)

    qk_rows, v_rows, context, log_total, attn_part = attend_fwd(
        count_cell, hidden_in, qk_full, vo_full, qk_bias, v_bias, text_len
    )
    attn_mine, attn_got = core_halves(attn_part)
    attn_got, up_near, down_side = lax.optimization_barrier((attn_got, up_near, down_side))
    up_full = gather_side(up_near).reshape(2, width, hidden)
    down_full = join(down_side, swap_docs(down_side, 0), docs_bit(0), 2).reshape(2, width, hidden)
    pre_one = my_rows(inputs) + (attn_mine + attn_got.astype(full) + bias_out)
    normed_one, scaled_one, inv_one = norm_forward(pre_one, gain_one, shift_one)
    normed_low = gather_core(normed_one.astype(low))
    activated, slope, down_part = ffn_fwd(normed_low, up_full, down_full, hidden_bias)
    grad_rows_out = lax.dynamic_slice_in_dim(
        cotangent, side * seq_len + row_start, half, 0
    ).astype(full)
    pre_two = normed_one + (reduce_core(down_part) + bias_down)
    normed_two, scaled_two, inv_two = norm_forward(pre_two, gain_two, shift_two)
    layer_out = normed_two.astype(low)
    grad_pre_two = norm_backward(grad_rows_out, scaled_two, inv_two, gain_two)
    gain_two_part = jnp.sum(grad_rows_out * scaled_two, axis=0)
    shift_two_part = jnp.sum(grad_rows_out, axis=0)
    grad_down_half = grad_pre_two.astype(low)
    bias_down_part = jnp.sum(grad_down_half.astype(full), axis=0)
    grad_down_low = gather_core(grad_down_half)
    grad_weight_up, grad_weight_down, bias_up_part, grad_normed_part = ffn_bwd(
        normed_low, grad_down_low, up_full, down_full, activated, slope
    )
    def split_docs(parts, stage, axis):
        bit = docs_bit(stage)
        theirs = lax.dynamic_index_in_dim(parts, 1 - bit, axis, keepdims=False).astype(low)
        return lax.dynamic_index_in_dim(parts, bit, axis, keepdims=False), theirs

    def split_side(parts):
        theirs = lax.dynamic_index_in_dim(parts, 1 - side, 0, keepdims=False).astype(low)
        return lax.dynamic_index_in_dim(parts, side, 0, keepdims=False), theirs

    def exchange(pieces, move):
        mine, theirs = pieces
        return mine.astype(full) + move(theirs).astype(full)

    def exchange_with(pieces, sums, move):
        mine, theirs = pieces
        lanes = theirs.shape[-1]
        sums = sums.reshape(-1, lanes).astype(low)
        flat = theirs.reshape(-1, lanes)
        got = move(jnp.concatenate([flat, sums], axis=0))
        cut = flat.shape[0]
        return (
            mine.astype(full) + got[:cut].reshape(mine.shape).astype(full),
            sums.astype(full) + got[cut:].astype(full),
        )

    def far_axis(stage):
        return stages - 1 - stage

    near_cut = (2, docs_size // 2, 2, block)
    far_cut = (2,) * (stages - 1) + (block,)

    up_mine, up_theirs = split_docs(grad_weight_up.reshape(near_cut + (hidden,)), 0, 2)
    down_mine, down_theirs = split_side(grad_weight_down.reshape(near_cut + (hidden,)))
    grad_normed_part, up_theirs, down_theirs = lax.optimization_barrier(
        (grad_normed_part, up_theirs, down_theirs)
    )
    up_got = swap_docs(up_theirs, 0)
    down_got = swap_side(down_theirs)
    grad_normed = reduce_core(grad_normed_part) + grad_pre_two
    grad_pre_one = norm_backward(grad_normed, scaled_one, inv_one, gain_one)
    gain_one_part = jnp.sum(grad_normed * scaled_one, axis=0)
    shift_one_part = jnp.sum(grad_normed, axis=0)
    grad_branch_half = grad_pre_one.astype(low)
    bias_out_part = jnp.sum(grad_branch_half.astype(full), axis=0)
    grad_branch_low = gather_core(grad_branch_half)
    grad_weight_qk, grad_weight_vo, bias_qk_part, bias_v_part, grad_hidden_part = attend_bwd(
        count_cell,
        hidden_in,
        grad_branch_low,
        qk_full,
        vo_full,
        qk_rows,
        v_rows,
        context,
        log_total,
        text_len,
    )
    grad_weight_qk, grad_weight_vo, up_got, down_got = lax.optimization_barrier(
        (grad_weight_qk, grad_weight_vo, up_got, down_got)
    )
    grad_inputs = (reduce_core(grad_hidden_part) + grad_pre_one).astype(low)
    up_parts = up_mine.astype(full) + up_got.astype(full)
    down_parts = down_mine.astype(full) + down_got.astype(full)
    up_parts = exchange(split_side(up_parts), swap_side)
    down_parts = exchange(split_docs(down_parts, 0, 1), lambda send: swap_docs(send, 0))
    total_ffn = jnp.concatenate([up_parts, down_parts], axis=-1).reshape(far_cut + (2 * hidden,))
    for stage in range(1, stages):
        total_ffn = exchange(
            split_docs(total_ffn, stage, far_axis(stage)), lambda send: swap_docs(send, stage)
        )

    sums = jnp.concatenate(
        [
            bias_qk_part.reshape(-1),
            bias_v_part.reshape(-1),
            bias_up_part.reshape(-1),
            bias_out_part,
            bias_down_part,
            gain_one_part,
            shift_one_part,
            gain_two_part,
            shift_two_part,
        ]
    )
    used = sums.shape[0]
    sums = jnp.concatenate([sums, jnp.zeros((-used % (16 * pair),), full)])
    qk_parts = grad_weight_qk.reshape(near_cut + (pair,))
    vo_parts = grad_weight_vo.reshape(near_cut + (pair,))
    qk_parts, sums = exchange_with(
        split_docs(qk_parts, 0, 2), sums, lambda send: swap_docs(send, 0)
    )
    vo_parts = exchange(split_side(vo_parts), swap_side)
    qk_parts, sums = exchange_with(split_side(qk_parts), sums, swap_side)
    vo_parts = exchange(split_docs(vo_parts, 0, 1), lambda send: swap_docs(send, 0))
    grad_inputs = lax.optimization_barrier((grad_inputs, qk_parts, vo_parts))[0]
    grad_sides = join(grad_inputs, swap_side(grad_inputs), side, 0)
    grad_all = join(grad_sides, swap_core(grad_sides), core, 1).reshape(2, seq_len, width)
    grad_all = lax.optimization_barrier(grad_all).astype(full)
    onehot_both = (seg_index[:, :, None] == slot_ids[None, None, :]).astype(full)
    divisor_both = jnp.maximum(jnp.sum(onehot_both, axis=1), 1.0)[:, :, None]
    live_both = (slot_ids[None, :] < seg_count[:, None]).astype(full)[:, :, None]
    grad_slots = live_both * grad_all[:, text_len:]
    spread_back = jnp.einsum(
        "gts,gsd->gtd",
        onehot_both,
        grad_slots / divisor_both,
        precision=lax.Precision.HIGHEST,
        preferred_element_type=full,
    )
    grad_tokens = (
        jnp.concatenate([grad_all[:, :text_len] + spread_back, grad_slots], axis=1)
        .reshape(2 * seq_len, width)
        .astype(low)
    )

    total_attn = jnp.concatenate([qk_parts, vo_parts], axis=-1).reshape(far_cut + (2 * pair,))
    for stage in range(1, stages):
        total_attn, sums = exchange_with(
            split_docs(total_attn, stage, far_axis(stage)),
            sums,
            lambda send: swap_docs(send, stage),
        )
    sums = sums.reshape(-1)
    ends = [2 * pair, 2 * pair + 512, 2 * pair + 512 + 2 * hidden]
    shared = sums[ends[2] : used]
    shared = (shared + swap_core(shared)).reshape(-1, width)

    def own_side(vector):
        return lax.dynamic_index_in_dim(vector.reshape(2, -1), side, 0, keepdims=False)

    gradient_query, gradient_key = unpack(total_attn[:, :pair])
    gradient_value, gradient_out = unpack(total_attn[:, pair:])
    return (
        layer_out,
        grad_tokens,
        gradient_query,
        gradient_key,
        gradient_value,
        gradient_out.T,
        total_ffn[:, :hidden],
        total_ffn[:, hidden:].T,
        unpack(own_side(sums[: ends[0]]))[0],
        own_side(sums[ends[0] : ends[1]])[:slab],
        shared[0],
        own_side(sums[ends[1] : ends[2]]),
        shared[1],
        shared[2],
        shared[3],
        shared[4],
        shared[5],
    )


def solution(mesh):
    placed = (
        P("docs", None),
        P("docs", None),
        P("docs"),
        P("docs", "heads"),
        P("docs", "heads"),
        P("docs", "heads"),
        P("heads", "docs"),
        P("docs", "heads"),
        P("heads", "docs"),
        P("heads"),
        P("heads"),
        P(),
        P("heads"),
        P(),
        P(),
        P(),
        P(),
        P(),
        P("docs", None),
    )
    return jax.shard_map(
        body,
        mesh=mesh,
        in_specs=placed,
        out_specs=(
            P(("docs", "heads"), None),
            P("docs", None),
            P("docs", "heads"),
            P("docs", "heads"),
            P("docs", "heads"),
            P("heads", "docs"),
            P("docs", "heads"),
            P("heads", "docs"),
            P("heads"),
            P("heads"),
            P(),
            P("heads"),
            P(),
            P(),
            P(),
            P(),
            P(),
        ),
        check_vma=False,
    )
```
